32 devices in a mesh: seq: 8 (over z, y), pack: 4 (over x, core).
Axes of the slice: x: 2, y: 2, z: 4, core: 2. Of those that a mesh axis runs over, the one named last changes fastest.
Arguments:
- queries: bfloat16 [8192, 2048], P(('pack', 'seq')), parts along dimension 0, may hold values from -10 to 10
- keys: bfloat16 [8192, 512], P(('pack', 'seq')), parts along dimension 0, may hold values from -10 to 10
- values: bfloat16 [8192, 512], P(('pack', 'seq')), parts along dimension 0, may hold values from -6 to 6
- lengths: int32 [32], P('pack'), parts along dimension 0, may hold values from 1 to 1024, 2048 in all
- home: int32 [64], P('pack'), parts along dimension 0, may hold values from 0 to 7, as said below
Outputs:
- attended: bfloat16 [8192, 2048], P(('pack', 'seq')), parts along dimension 0
The draws below stay inside these ranges and needn't reach their ends.
There are 4 independent parts, one for each index of `pack`. The reference program is written for one: setup_inputs(seed, part) draws one part's arguments, and reference() takes and returns one part's arrays. A program takes and returns all parts, laid end to end along the dimension named above; each array names one. Nothing has to cross between parts.
Inputs may be any that keep to these rules, and one draw needn't show every extreme that they name: Block b covers positions b * 128 to b * 128 + 127. home[b] is 2 * (b // 4) or that plus one, and every device index is home of exactly 2 blocks.
All inputs are finite; a program needn't handle non-finite values.
Results may differ from the reference program's by a relative error of at most 0.0033.
Values may be sent and summed in bfloat16 or wider, within the bound.
A program may use at most 64 MiB of HBM per device.

```python
import math
import jax
import jax.numpy as jnp
import numpy as np
from jax import lax

QH = 16
KVH = 4
HD = 128
BLOCK = 128
GROUP = 4
WINDOW = 2048
TOKENS = 2048
DOCS = 8
MOST_LEN = 1024
NBLK = 16
BPD = 2


def draw_queries(key, part):
    normal_part = jnp.clip(jax.random.normal(jax.random.fold_in(key, 11), (TOKENS, QH * HD), jnp.float32), -6.0, 6.0)
    return normal_part.astype(jnp.bfloat16)


def draw_keys(key, part):
    normal_part = jnp.clip(jax.random.normal(jax.random.fold_in(key, 12), (TOKENS, KVH * HD), jnp.float32), -6.0, 6.0)
    return normal_part.astype(jnp.bfloat16)


def draw_home(key, part):
    group_count = NBLK // (2 * BPD)
    group_keys = jax.random.split(jax.random.fold_in(key, 21), group_count)
    shuffles = jax.vmap(lambda one_key: jax.random.permutation(one_key, 2 * BPD))(group_keys)
    ranking = jnp.argsort(shuffles, axis=1, stable=True).astype(jnp.int32)
    group_ids = jnp.arange(group_count, dtype=jnp.int32)[:, None]
    home = 2 * group_ids + (ranking >= BPD).astype(jnp.int32)
    return home.reshape(NBLK).astype(jnp.int32)


def block_levels(key, dims, shards, least, top_value):
    def one(axis_at, shards_of):
        heights = jax.random.uniform(jax.random.fold_in(jax.random.fold_in(key, 6), axis_at), (shards_of,), jnp.float32, least / len(shards), top_value / len(shards))
        return jnp.repeat(jnp.exp(heights), dims[axis_at] // shards_of).reshape((-1,) + (1,) * (len(dims) - axis_at - 1))

    level = one(*shards[0])
    for cut in shards[1:]:
        level = level * one(*cut)
    return level


def split_up(amount, total, reach, lean):
    weights = [(1 << 20) // math.isqrt(standing ** lean) + 1 for standing in range(2, amount + 1)]
    rest, counts = total - reach - (amount - 1), [1] * (amount - 1)
    while rest > 0:
        movable = [i for i in range(amount - 1) if counts[i] < reach]
        pool, left = sum([weights[i] for i in movable]), rest
        for i in movable:
            extra = min(reach - counts[i], max(1, left * weights[i] // pool), rest)
            counts[i] = counts[i] + extra
            rest = rest - extra
    return np.array([reach] + counts)


def uneven(stream_key, count, total, bound, skew):
    if count == 2:
        one = jax.random.randint(stream_key, (), max(1, total - bound), min(bound, total - 1) + 1)
        return jnp.stack([one, total - one])
    sizes = jnp.asarray(split_up(count, total, bound, skew), jnp.int32)
    twos = (count - 1) // 2
    giver, taker = sizes[1:1 + 2 * twos:2], sizes[2:2 + 2 * twos:2]
    margin = jnp.minimum(giver - 1, bound - taker)
    moved = jax.random.randint(jax.random.fold_in(stream_key, 1), (twos,), 0, 1 << 20) % (margin + 1)
    sizes = sizes.at[1:1 + 2 * twos:2].set(giver - moved).at[2:2 + 2 * twos:2].set(taker + moved)
    return sizes[jax.random.permutation(jax.random.fold_in(stream_key, 2), count)]


def gaussian(own_key, dims, deviation, reach, shards=(), kind=jnp.bfloat16):
    drawn = jax.random.normal(own_key, dims, jnp.float32) * deviation
    if len(shards) > 0:
        drawn = block_levels(own_key, dims, shards, -0.22, 0.18) * drawn
    return jnp.clip(drawn, min=-reach, max=reach).astype(kind)


def setup_inputs(seed: int = 0, part: int = 0) -> dict:
    arg_keys = jax.random.split(jax.random.key(seed), 6)
    part_keys = jax.random.split(jax.random.fold_in(arg_keys[5], part), 6)
    queries = draw_queries(jax.random.fold_in(jax.random.fold_in(arg_keys[5], part), 71), part)
    keys = draw_keys(jax.random.fold_in(jax.random.fold_in(arg_keys[5], part), 71), part)
    values = gaussian(part_keys[2], (TOKENS, KVH * HD), 1.0, 6.0, ((0, 8),))
    lengths = uneven(part_keys[3], DOCS, TOKENS, MOST_LEN, 2).astype(jnp.int32)
    home = draw_home(jax.random.fold_in(jax.random.fold_in(arg_keys[5], part), 71), part)
    return dict(queries=queries, keys=keys, values=values, lengths=lengths, home=home)


def doc_first_of(lengths, positions):
    doc_ends = jnp.cumsum(lengths).astype(jnp.int32)
    doc_starts = (doc_ends - lengths).astype(jnp.int32)
    chosen = jnp.where(doc_starts[None, :] <= positions[:, None], doc_starts[None, :], 0)
    return jnp.max(chosen, axis=1).astype(jnp.int32)


def reference(queries, keys, values, lengths, home):
    positions = jnp.arange(TOKENS, dtype=jnp.int32)
    doc_first = doc_first_of(lengths, positions)
    zero_rows = jnp.zeros((WINDOW, KVH * HD), jnp.bfloat16)
    keys_padded = jnp.concatenate([zero_rows, keys], axis=0)
    values_padded = jnp.concatenate([zero_rows, values], axis=0)

    def one_block(block_id):
        row_start = (block_id * BLOCK).astype(jnp.int32)
        query_rows = lax.dynamic_slice_in_dim(queries, row_start, BLOCK, 0).astype(jnp.float32).reshape(BLOCK, KVH, GROUP, HD)
        key_rows = lax.dynamic_slice_in_dim(keys_padded, row_start, WINDOW + BLOCK, 0).astype(jnp.float32).reshape(WINDOW + BLOCK, KVH, HD)
        value_rows = lax.dynamic_slice_in_dim(values_padded, row_start, WINDOW + BLOCK, 0).astype(jnp.float32).reshape(WINDOW + BLOCK, KVH, HD)
        query_pos = row_start + jnp.arange(BLOCK, dtype=jnp.int32)
        key_pos = row_start - WINDOW + jnp.arange(WINDOW + BLOCK, dtype=jnp.int32)
        first_rows = lax.dynamic_slice_in_dim(doc_first, row_start, BLOCK, 0)
        allowed = (key_pos[None, :] <= query_pos[:, None]) & (key_pos[None, :] > query_pos[:, None] - WINDOW) & (key_pos[None, :] >= first_rows[:, None])
        scores = jnp.einsum("qhgd,khd->hgqk", query_rows, key_rows) * (HD ** -0.5)
        scores = jnp.where(allowed, scores, jnp.float32(-1e30))
        row_max = jnp.max(scores, axis=-1, keepdims=True)
        weights = jnp.where(allowed, jnp.exp(scores - row_max), jnp.float32(0.0))
        denominator = jnp.sum(weights, axis=-1)
        rounded = lax.optimization_barrier(weights.astype(jnp.bfloat16)).astype(jnp.float32)
        numerator = jnp.einsum("hgqk,khd->hgqd", rounded, value_rows)
        mixed = numerator / denominator[..., None]
        return mixed.transpose(2, 0, 1, 3).reshape(BLOCK, QH * HD).astype(jnp.bfloat16)

    block_outputs = lax.map(one_block, jnp.arange(NBLK, dtype=jnp.int32))
    slot_order = jnp.argsort(home, stable=True).astype(jnp.int32)
    return block_outputs[slot_order].reshape(TOKENS, QH * HD)
```

```python
import functools

import jax
import jax.numpy as jnp
from jax import lax
from jax.experimental import pallas as pl
from jax.experimental.pallas import tpu as pltpu
from jax.sharding import PartitionSpec as P

HD = 128
BLOCK = 128
WINDOW = 2048
LOG2E = 1.4426950408889634
FAR = float(2**20)
MESH = pl.DeviceIdType.MESH


def spans(row_block, depth, blocks, reach):
    found = []
    for back in range(depth, -1, -1):
        near = [
            kb
            for kb in range(blocks)
            if -BLOCK < (back * blocks + row_block - kb) * BLOCK < reach + BLOCK - 1
        ]
        if near:
            found.append((back, near[0], near[-1] + 1))
    return found


def fused(
    plan, lengths, home, queries, keys, values, out,
    q, kv, qext, kext, mixed, give, keep,
    load_sem, q_load, q_send, q_recv, kv_send, kv_recv, hop_send, hop_recv, o_send, o_recv, o_keep,
):
    group, halves, depth, reach, windowed, chunk = plan
    rows = queries.shape[0]
    blocks = 2 * rows // BLOCK
    per = blocks // 2
    me = lax.axis_index("seq")
    count = lax.axis_size("seq")
    other = me ^ 1
    parity = me % 2
    pair = me // 2
    last = count // 2 - 1
    scale = HD ** (-0.5) * LOG2E

    def columns(head, wide=1):
        return pl.ds(pl.multiple_of(head * HD, HD), wide * HD)

    def load_kv(h, t):
        source = keys if t == 0 else values
        return pltpu.make_async_copy(
            source.at[:, columns(parity * halves + h)], kv.at[h, t, 0, parity], load_sem.at[h, t]
        )

    def load_q(h, g):
        return pltpu.make_async_copy(
            queries.at[:, columns((parity * halves + h) * group + g)],
            q.at[h, g, parity],
            q_load.at[h, g],
        )

    def swap_kv(h, t):
        source = keys if t == 0 else values
        return pltpu.make_async_remote_copy(
            source.at[:, columns((1 - parity) * halves + h)],
            kv.at[h, t, 0, parity],
            kv_send.at[h, t],
            kv_recv.at[h, t],
            device_id={"seq": other},
            device_id_type=MESH,
        )

    def swap_q(h, g):
        return pltpu.make_async_remote_copy(
            queries.at[:, columns(((1 - parity) * halves + h) * group + g)],
            q.at[h, g, parity],
            q_send.at[h, g],
            q_recv.at[h, g],
            device_id={"seq": other},
            device_id_type=MESH,
        )

    def hop(h, back, side):
        return pltpu.make_async_remote_copy(
            kv.at[h, :, back, side],
            kv.at[h, :, back + 1, side],
            hop_send.at[h, back, side],
            hop_recv.at[h, back, side],
            device_id={"seq": me + 2},
            device_id_type=MESH,
        )

    def send_out(h, g):
        return pltpu.make_async_remote_copy(
            give.at[h, g],
            out.at[:, columns((parity * halves + h) * group + g)],
            o_send.at[h, g],
            o_recv.at[h, g],
            device_id={"seq": other},
            device_id_type=MESH,
        )

    def keep_out(h, g):
        return pltpu.make_async_copy(
            keep.at[h, g], out.at[:, columns((parity * halves + h) * group + g)], o_keep.at[h, g]
        )

    def forward(h, back, side):
        if back > 0:

            @pl.when(pair >= back)
            def _():
                hop(h, back - 1, side).wait_recv()

        if back < depth:

            @pl.when((pair >= back) & (pair < last))
            def _():
                hop(h, back, side).start()

    for h in range(halves):
        for t in range(2):
            load_kv(h, t).start()
    for h in range(halves):
        for g in range(group):
            load_q(h, g).start()

    barrier = pltpu.get_barrier_semaphore()
    pl.semaphore_signal(barrier, inc=1, device_id={"seq": other}, device_id_type=MESH)

    @pl.when(pair > 0)
    def _():
        pl.semaphore_signal(barrier, inc=1, device_id={"seq": me - 2}, device_id_type=MESH)

    pl.semaphore_wait(barrier, 1 + (pair < last).astype(jnp.int32))

    for h in range(halves):
        for t in range(2):
            swap_kv(h, t).start()
    for h in range(halves):
        for t in range(2):
            load_kv(h, t).wait()
        forward(h, 0, parity)
    for h in range(halves):
        for g in range(group):
            swap_q(h, g).start()

    docs = lengths.shape[0]
    lane = lax.broadcasted_iota(jnp.int32, (8, HD), 1)

    def add_doc(doc, state):
        begin, starts, ends = state
        end = begin + lengths[doc]
        here = lane == doc
        return end, jnp.where(here, begin, starts), jnp.where(here, end, ends)

    nothing = jnp.zeros((8, HD), jnp.int32)
    _, starts, ends = lax.fori_loop(
        0, docs, add_doc, (jnp.int32(0), nothing, nothing), unroll=docs <= 16
    )
    starts, ends = starts[:1], ends[:1]
    offset = lax.broadcasted_iota(jnp.int32, (2 * rows, HD), 0)
    for back in range(depth + 1):
        position = (pair - back) * 2 * rows + offset
        inside = ((position >= starts) & (position < ends)) | (position < 0)
        kext[back] = jnp.where(inside, 1.0, 0.0).astype(kext.dtype)
        if back == 0:
            qext[...] = jnp.where(inside, 0.0, -FAR).astype(qext.dtype)
        else:

            @pl.when(pair < back)
            def _():
                for h in range(halves):
                    kv[h, :, back] = jnp.zeros(kv.shape[1:2] + kv.shape[3:], kv.dtype)

    mine = [(home[pair * blocks + b] == me).astype(jnp.int32) for b in range(blocks)]
    kept_at = [jnp.int32(0)] * per
    sent_at = [jnp.int32(0)] * per
    kept_count, sent_count = jnp.int32(0), jnp.int32(0)
    for b in range(blocks):
        for s in range(per):
            kept_at[s] = jnp.where((mine[b] == 1) & (kept_count == s), b, kept_at[s])
            sent_at[s] = jnp.where((mine[b] == 0) & (sent_count == s), b, sent_at[s])
        kept_count = kept_count + mine[b]
        sent_count = sent_count + 1 - mine[b]

    def take_swapped(h):
        for t in range(2):
            swap_kv(h, t).wait_recv()
        forward(h, 0, 1 - parity)

    def keys_of(h, t, back, low, high):
        joined = kv[h, t, back].reshape(2 * rows, HD)
        return joined[low * BLOCK : high * BLOCK]

    def attend(h, first):
        for j in range(blocks):
            side, inner = j // per, j % per
            runs = spans(j, depth, blocks, reach)
            at = pl.ds(inner * BLOCK, BLOCK)
            block = jnp.concatenate([q[h, first + g, side, at] for g in range(chunk)], axis=0)
            extra = jnp.concatenate([qext[pl.ds(j * BLOCK, BLOCK)]] * chunk, axis=0)
            grouped = jnp.concatenate([block, extra], axis=1)
            seen = jnp.concatenate(
                [
                    jnp.concatenate(
                        [keys_of(h, 0, back, low, high), kext[back, low * BLOCK : high * BLOCK]],
                        axis=1,
                    )
                    for back, low, high in runs
                ],
                axis=0,
            )
            raw = lax.dot_general(
                grouped, seen, (((1,), (1,)), ((), ())), preferred_element_type=jnp.float32
            )
            parts = []
            begin = 0
            for back, low, high in runs:
                for kb in range(low, high):
                    part = raw[:, begin : begin + BLOCK]
                    begin += BLOCK
                    gap = (back * blocks + j - kb) * BLOCK
                    row = lax.broadcasted_iota(jnp.int32, (BLOCK, BLOCK), 0)
                    column = lax.broadcasted_iota(jnp.int32, (BLOCK, BLOCK), 1)
                    allowed = None
                    if gap < BLOCK:
                        allowed = gap + row >= column
                    if windowed and gap + BLOCK > WINDOW:
                        allowed = gap + row - column < WINDOW
                    if allowed is not None:
                        shaped = part.reshape(chunk, BLOCK, BLOCK)
                        part = jnp.where(allowed[None], shaped, -FAR).reshape(part.shape)
                    parts.append(part)
            peak = parts[0]
            for part in parts[1:]:
                peak = jnp.maximum(peak, part)
            peak = jnp.max(peak, axis=1, keepdims=True)
            weights = jnp.concatenate(
                [jnp.exp2((part - peak) * scale).astype(jnp.bfloat16) for part in parts], axis=1
            )
            joined = jnp.concatenate(
                [keys_of(h, 1, back, low, high) for back, low, high in runs], axis=0
            )
            joined = jnp.concatenate([joined, jnp.ones_like(joined)], axis=1)
            both = jnp.dot(weights, joined, preferred_element_type=jnp.float32)
            result = (both[:, :HD] / both[:, HD:]).astype(mixed.dtype)
            for g in range(chunk):
                mixed[h, first + g, j] = result[g * BLOCK : (g + 1) * BLOCK]

    def deliver(h, first):
        for g in range(chunk):
            for s in range(per):
                give[h, first + g, pl.ds(s * BLOCK, BLOCK)] = mixed[h, first + g, sent_at[s]]
                keep[h, first + g, pl.ds(s * BLOCK, BLOCK)] = mixed[h, first + g, kept_at[s]]
            send_out(h, first + g).start()
            keep_out(h, first + g).start()

    def settle(h):
        for g in range(group):
            load_q(h, g).wait()
            swap_q(h, g).wait_recv()

    for h in range(halves):
        take_swapped(h)
        if h == 0:
            for back in range(1, depth + 1):
                forward(h, back, parity)
                forward(h, back, 1 - parity)
    for h in range(halves):
        settle(h)
        if h > 0:
            for back in range(1, depth + 1):
                forward(h, back, parity)
                forward(h, back, 1 - parity)

        @pl.loop(0, group // chunk)
        def _(step):
            attend(h, step * chunk)
            deliver(h, step * chunk)

    for h in range(halves):
        for t in range(2):
            swap_kv(h, t).wait_send()
        for back in range(depth):
            for side in range(2):

                @pl.when((pair >= back) & (pair < last))
                def _():
                    hop(h, back, side).wait_send()

        for g in range(group):
            swap_q(h, g).wait_send()
            keep_out(h, g).wait()
            send_out(h, g).wait()


def local(queries, keys, values, lengths, home):
    rows, query_cols = queries.shape
    kv_heads = keys.shape[1] // HD
    group = query_cols // HD // kv_heads
    halves = kv_heads // 2
    blocks = 2 * rows // BLOCK
    seq = lax.axis_size("seq")
    tokens = seq * rows
    most_len = min(tokens // 2, 4096)
    reach = min(WINDOW, most_len)
    depth = min(-(-(reach - 1) // (2 * rows)), seq // 2 - 1)
    plan = (group, halves, depth, reach, most_len > WINDOW, 2)
    bf16 = jnp.bfloat16
    dma = pltpu.SemaphoreType.DMA
    anywhere = pl.BlockSpec(memory_space=pl.ANY)
    smem = pl.BlockSpec(memory_space=pltpu.SMEM)
    return pl.pallas_call(
        functools.partial(fused, plan),
        out_shape=jax.ShapeDtypeStruct(queries.shape, bf16),
        in_specs=[smem, smem, anywhere, anywhere, anywhere],
        out_specs=anywhere,
        scratch_shapes=[
            pltpu.VMEM((halves, group, 2, rows, HD), bf16),
            pltpu.VMEM((halves, 2, depth + 1, 2, rows, HD), bf16),
            pltpu.VMEM((2 * rows, HD), bf16),
            pltpu.VMEM((depth + 1, 2 * rows, HD), bf16),
            pltpu.VMEM((halves, group, blocks, BLOCK, HD), bf16),
            pltpu.VMEM((halves, group, rows, HD), bf16),
            pltpu.VMEM((halves, group, rows, HD), bf16),
            dma((halves, 2)),
            dma((halves, group)),
            dma((halves, group)),
            dma((halves, group)),
            dma((halves, 2)),
            dma((halves, 2)),
            dma((halves, depth, 2)),
            dma((halves, depth, 2)),
            dma((halves, group)),
            dma((halves, group)),
            dma((halves, group)),
        ],
        compiler_params=pltpu.CompilerParams(
            collective_id=0, has_side_effects=True, vmem_limit_bytes=48 * 1024 * 1024
        ),
    )(lengths, home, queries, keys, values)


def solution(mesh):
    placed = (
        P(("pack", "seq"), None),
        P(("pack", "seq"), None),
        P(("pack", "seq"), None),
        P("pack"),
        P("pack"),
    )
    return jax.shard_map(
        local, mesh=mesh, in_specs=placed, out_specs=P(("pack", "seq"), None), check_vma=False
    )
```

```python
import functools

import jax
import jax.numpy as jnp
from jax import lax
from jax.experimental import pallas as pl
from jax.experimental.pallas import tpu as pltpu
from jax.sharding import PartitionSpec as P

HD = 128
BLOCK = 128
WINDOW = 2048
LOG2E = 1.4426950408889634
FAR = float(2**20)
MESH = pl.DeviceIdType.MESH


def spans(row_block, depth, blocks, reach):
    found = []
    for back in range(depth, -1, -1):
        near = [
            kb
            for kb in range(blocks)
            if -BLOCK < (back * blocks + row_block - kb) * BLOCK < reach + BLOCK - 1
        ]
        if near:
            found.append((back, near[0], near[-1] + 1))
    return found


def fused(
    plan, lengths_in, home_in, queries, keys, values, out,
    lengths, home, q, kv, qext, kext, mixed, give, keep,
    small_sem, load_sem, q_load, q_send, q_recv, kv_send, kv_recv, hop_send, hop_recv, o_send, o_recv, o_keep,
):
    group, halves, depth, reach, windowed, chunk = plan
    rows = queries.shape[0]
    blocks = 2 * rows // BLOCK
    per = blocks // 2
    me = lax.axis_index("seq")
    count = lax.axis_size("seq")
    other = me ^ 1
    parity = me % 2
    pair = me // 2
    last = count // 2 - 1
    scale = HD ** (-0.5) * LOG2E

    def columns(head, wide=1):
        return pl.ds(pl.multiple_of(head * HD, HD), wide * HD)

    def load_kv(h, t):
        source = keys if t == 0 else values
        return pltpu.make_async_copy(
            source.at[:, columns(parity * halves + h)], kv.at[h, t, 0, parity], load_sem.at[h, t]
        )

    def load_q(h, g):
        return pltpu.make_async_copy(
            queries.at[:, columns((parity * halves + h) * group + g)],
            q.at[h, g, parity],
            q_load.at[h, g],
        )

    def swap_kv(h, t):
        source = keys if t == 0 else values
        return pltpu.make_async_remote_copy(
            source.at[:, columns((1 - parity) * halves + h)],
            kv.at[h, t, 0, parity],
            kv_send.at[h, t],
            kv_recv.at[h, t],
            device_id={"seq": other},
            device_id_type=MESH,
        )

    def swap_q(h, g):
        return pltpu.make_async_remote_copy(
            queries.at[:, columns(((1 - parity) * halves + h) * group + g)],
            q.at[h, g, parity],
            q_send.at[h, g],
            q_recv.at[h, g],
            device_id={"seq": other},
            device_id_type=MESH,
        )

    def hop(h, back, side):
        return pltpu.make_async_remote_copy(
            kv.at[h, :, back, side],
            kv.at[h, :, back + 1, side],
            hop_send.at[h, back, side],
            hop_recv.at[h, back, side],
            device_id={"seq": me + 2},
            device_id_type=MESH,
        )

    def send_out(h, g):
        return pltpu.make_async_remote_copy(
            give.at[h, g],
            out.at[:, columns((parity * halves + h) * group + g)],
            o_send.at[h, g],
            o_recv.at[h, g],
            device_id={"seq": other},
            device_id_type=MESH,
        )

    def keep_out(h, g):
        return pltpu.make_async_copy(
            keep.at[h, g], out.at[:, columns((parity * halves + h) * group + g)], o_keep.at[h, g]
        )

    def forward(h, back, side):
        if back > 0:

            @pl.when(pair >= back)
            def _():
                hop(h, back - 1, side).wait_recv()

        if back < depth:

            @pl.when((pair >= back) & (pair < last))
            def _():
                hop(h, back, side).start()

    small = [
        pltpu.make_async_copy(lengths_in, lengths, small_sem.at[0]),
        pltpu.make_async_copy(home_in, home, small_sem.at[1]),
    ]
    for h in range(halves):
        for t in range(2):
            load_kv(h, t).start()
    for copy in small:
        copy.start()
    for h in range(halves):
        for g in range(group):
            load_q(h, g).start()

    barrier = pltpu.get_barrier_semaphore()
    pl.semaphore_signal(barrier, inc=1, device_id={"seq": other}, device_id_type=MESH)

    @pl.when(pair > 0)
    def _():
        pl.semaphore_signal(barrier, inc=1, device_id={"seq": me - 2}, device_id_type=MESH)

    pl.semaphore_wait(barrier, 1 + (pair < last).astype(jnp.int32))

    for h in range(halves):
        for t in range(2):
            swap_kv(h, t).start()
    for h in range(halves):
        for t in range(2):
            load_kv(h, t).wait()
        forward(h, 0, parity)
    for h in range(halves):
        for g in range(group):
            swap_q(h, g).start()

    for copy in small:
        copy.wait()

    docs = lengths.shape[0]
    lane = lax.broadcasted_iota(jnp.int32, (8, HD), 1)

    def add_doc(doc, state):
        begin, starts, ends = state
        end = begin + lengths[doc]
        here = lane == doc
        return end, jnp.where(here, begin, starts), jnp.where(here, end, ends)

    nothing = jnp.zeros((8, HD), jnp.int32)
    _, starts, ends = lax.fori_loop(
        0, docs, add_doc, (jnp.int32(0), nothing, nothing), unroll=docs <= 16
    )
    starts, ends = starts[:1], ends[:1]
    offset = lax.broadcasted_iota(jnp.int32, (2 * rows, HD), 0)
    for back in range(depth + 1):
        position = (pair - back) * 2 * rows + offset
        inside = ((position >= starts) & (position < ends)) | (position < 0)
        kext[back] = jnp.where(inside, 1.0, 0.0).astype(kext.dtype)
        if back == 0:
            qext[...] = jnp.where(inside, 0.0, -FAR).astype(qext.dtype)
        else:

            @pl.when(pair < back)
            def _():
                for h in range(halves):
                    kv[h, :, back] = jnp.zeros(kv.shape[1:2] + kv.shape[3:], kv.dtype)

    mine = [(home[pair * blocks + b] == me).astype(jnp.int32) for b in range(blocks)]
    kept_at = [jnp.int32(0)] * per
    sent_at = [jnp.int32(0)] * per
    kept_count, sent_count = jnp.int32(0), jnp.int32(0)
    for b in range(blocks):
        for s in range(per):
            kept_at[s] = jnp.where((mine[b] == 1) & (kept_count == s), b, kept_at[s])
            sent_at[s] = jnp.where((mine[b] == 0) & (sent_count == s), b, sent_at[s])
        kept_count = kept_count + mine[b]
        sent_count = sent_count + 1 - mine[b]

    def take_swapped(h):
        for t in range(2):
            swap_kv(h, t).wait_recv()
        forward(h, 0, 1 - parity)

    def keys_of(h, t, back, low, high):
        joined = kv[h, t, back].reshape(2 * rows, HD)
        return joined[low * BLOCK : high * BLOCK]

    def attend(h, first):
        for j in range(blocks):
            side, inner = j // per, j % per
            runs = spans(j, depth, blocks, reach)
            at = pl.ds(inner * BLOCK, BLOCK)
            block = jnp.concatenate([q[h, first + g, side, at] for g in range(chunk)], axis=0)
            extra = jnp.concatenate([qext[pl.ds(j * BLOCK, BLOCK)]] * chunk, axis=0)
            grouped = jnp.concatenate([block, extra], axis=1)
            seen = jnp.concatenate(
                [
                    jnp.concatenate(
                        [keys_of(h, 0, back, low, high), kext[back, low * BLOCK : high * BLOCK]],
                        axis=1,
                    )
                    for back, low, high in runs
                ],
                axis=0,
            )
            raw = lax.dot_general(
                grouped, seen, (((1,), (1,)), ((), ())), preferred_element_type=jnp.float32
            )
            parts = []
            begin = 0
            for back, low, high in runs:
                for kb in range(low, high):
                    part = raw[:, begin : begin + BLOCK]
                    begin += BLOCK
                    gap = (back * blocks + j - kb) * BLOCK
                    row = lax.broadcasted_iota(jnp.int32, (BLOCK, BLOCK), 0)
                    column = lax.broadcasted_iota(jnp.int32, (BLOCK, BLOCK), 1)
                    allowed = None
                    if gap < BLOCK:
                        allowed = gap + row >= column
                    if windowed and gap + BLOCK > WINDOW:
                        allowed = gap + row - column < WINDOW
                    if allowed is not None:
                        shaped = part.reshape(chunk, BLOCK, BLOCK)
                        part = jnp.where(allowed[None], shaped, -FAR).reshape(part.shape)
                    parts.append(part)
            peak = parts[0]
            for part in parts[1:]:
                peak = jnp.maximum(peak, part)
            peak = jnp.max(peak, axis=1, keepdims=True)
            weights = jnp.concatenate(
                [jnp.exp2((part - peak) * scale).astype(jnp.bfloat16) for part in parts], axis=1
            )
            joined = jnp.concatenate(
                [keys_of(h, 1, back, low, high) for back, low, high in runs], axis=0
            )
            joined = jnp.concatenate([joined, jnp.ones_like(joined)], axis=1)
            both = jnp.dot(weights, joined, preferred_element_type=jnp.float32)
            result = (both[:, :HD] / both[:, HD:]).astype(mixed.dtype)
            for g in range(chunk):
                mixed[h, first + g, j] = result[g * BLOCK : (g + 1) * BLOCK]

    def deliver(h, first):
        for g in range(chunk):
            for s in range(per):
                give[h, first + g, pl.ds(s * BLOCK, BLOCK)] = mixed[h, first + g, sent_at[s]]
                keep[h, first + g, pl.ds(s * BLOCK, BLOCK)] = mixed[h, first + g, kept_at[s]]
            send_out(h, first + g).start()
            keep_out(h, first + g).start()

    def settle(h):
        for g in range(group):
            load_q(h, g).wait()
            swap_q(h, g).wait_recv()

    for h in range(halves):
        take_swapped(h)
        if h == 0:
            for back in range(1, depth + 1):
                forward(h, back, parity)
                forward(h, back, 1 - parity)
    for h in range(halves):
        settle(h)
        if h > 0:
            for back in range(1, depth + 1):
                forward(h, back, parity)
                forward(h, back, 1 - parity)

        @pl.loop(0, group // chunk)
        def _(step):
            attend(h, step * chunk)
            deliver(h, step * chunk)

    for h in range(halves):
        for t in range(2):
            swap_kv(h, t).wait_send()
        for back in range(depth):
            for side in range(2):

                @pl.when((pair >= back) & (pair < last))
                def _():
                    hop(h, back, side).wait_send()

        for g in range(group):
            swap_q(h, g).wait_send()
            keep_out(h, g).wait()
            send_out(h, g).wait()


def local(queries, keys, values, lengths, home):
    rows, query_cols = queries.shape
    kv_heads = keys.shape[1] // HD
    group = query_cols // HD // kv_heads
    halves = kv_heads // 2
    blocks = 2 * rows // BLOCK
    seq = lax.axis_size("seq")
    tokens = seq * rows
    most_len = min(tokens // 2, 4096)
    reach = min(WINDOW, most_len)
    depth = min(-(-(reach - 1) // (2 * rows)), seq // 2 - 1)
    plan = (group, halves, depth, reach, most_len > WINDOW, 2)
    bf16 = jnp.bfloat16
    dma = pltpu.SemaphoreType.DMA
    anywhere = pl.BlockSpec(memory_space=pl.ANY)
    hbm = pl.BlockSpec(memory_space=pltpu.HBM)
    return pl.pallas_call(
        functools.partial(fused, plan),
        out_shape=pltpu.VMEM(queries.shape, bf16),
        in_specs=[hbm] * 5,
        out_specs=pl.BlockSpec(memory_space=pltpu.VMEM),
        scratch_shapes=[
            pltpu.SMEM(lengths.shape, jnp.int32),
            pltpu.SMEM(home.shape, jnp.int32),
            pltpu.VMEM((halves, group, 2, rows, HD), bf16),
            pltpu.VMEM((halves, 2, depth + 1, 2, rows, HD), bf16),
            pltpu.VMEM((2 * rows, HD), bf16),
            pltpu.VMEM((depth + 1, 2 * rows, HD), bf16),
            pltpu.VMEM((halves, group, blocks, BLOCK, HD), bf16),
            pltpu.VMEM((halves, group, rows, HD), bf16),
            pltpu.VMEM((halves, group, rows, HD), bf16),
            dma((2,)),
            dma((halves, 2)),
            dma((halves, group)),
            dma((halves, group)),
            dma((halves, group)),
            dma((halves, 2)),
            dma((halves, 2)),
            dma((halves, depth, 2)),
            dma((halves, depth, 2)),
            dma((halves, group)),
            dma((halves, group)),
            dma((halves, group)),
        ],
        compiler_params=pltpu.CompilerParams(
            collective_id=0, has_side_effects=True, vmem_limit_bytes=60 * 1024 * 1024
        ),
    )(lengths, home, queries, keys, values)


def solution(mesh):
    placed = (
        P(("pack", "seq"), None),
        P(("pack", "seq"), None),
        P(("pack", "seq"), None),
        P("pack"),
        P("pack"),
    )
    return jax.shard_map(
        local, mesh=mesh, in_specs=placed, out_specs=P(("pack", "seq"), None), check_vma=False
    )
```

```python
import functools

import jax
import jax.numpy as jnp
from jax import lax
from jax.experimental import pallas as pl
from jax.experimental.pallas import tpu as pltpu
from jax.sharding import PartitionSpec as P

HD = 128
BLOCK = 128
WINDOW = 2048
LOG2E = 1.4426950408889634
FAR = float(2**20)
MESH = pl.DeviceIdType.MESH


def spans(row_block, depth, blocks, reach):
    found = []
    for back in range(depth, -1, -1):
        near = [
            kb
            for kb in range(blocks)
            if -BLOCK < (back * blocks + row_block - kb) * BLOCK < reach + BLOCK - 1
        ]
        if near:
            found.append((back, near[0], near[-1] + 1))
    return found


def fused(
    plan, lengths_in, home_in, queries, keys, values, out,
    lengths, home, q, kv, qext, kext, mixed, give, keep, top, part_sum,
    small_sem, load_sem, q_load, q_send, q_recv, kv_send, kv_recv, hop_send, hop_recv, o_send, o_recv, o_keep,
):
    group, halves, depth, reach, windowed, chunk = plan
    rows = queries.shape[0]
    blocks = 2 * rows // BLOCK
    per = blocks // 2
    me = lax.axis_index("seq")
    count = lax.axis_size("seq")
    other = me ^ 1
    parity = me % 2
    pair = me // 2
    last = count // 2 - 1
    scale = HD ** (-0.5) * LOG2E

    def columns(head, wide=1):
        return pl.ds(pl.multiple_of(head * HD, HD), wide * HD)

    def load_kv(h, t):
        source = keys if t == 0 else values
        return pltpu.make_async_copy(
            source.at[:, columns(parity * halves + h)], kv.at[h, t, 0, parity], load_sem.at[h, t]
        )

    def load_q(h, g):
        return pltpu.make_async_copy(
            queries.at[:, columns((parity * halves + h) * group + g)],
            q.at[h, g, parity],
            q_load.at[h, g],
        )

    def swap_kv(h, t):
        source = keys if t == 0 else values
        return pltpu.make_async_remote_copy(
            source.at[:, columns((1 - parity) * halves + h)],
            kv.at[h, t, 0, parity],
            kv_send.at[h, t],
            kv_recv.at[h, t],
            device_id={"seq": other},
            device_id_type=MESH,
        )

    def swap_q(h, g):
        return pltpu.make_async_remote_copy(
            queries.at[:, columns(((1 - parity) * halves + h) * group + g)],
            q.at[h, g, parity],
            q_send.at[h, g],
            q_recv.at[h, g],
            device_id={"seq": other},
            device_id_type=MESH,
        )

    def hop(h, back, side):
        return pltpu.make_async_remote_copy(
            kv.at[h, :, back, side],
            kv.at[h, :, back + 1, side],
            hop_send.at[h, back, side],
            hop_recv.at[h, back, side],
            device_id={"seq": me + 2},
            device_id_type=MESH,
        )

    def send_out(h, g):
        return pltpu.make_async_remote_copy(
            give.at[h, g],
            out.at[:, columns((parity * halves + h) * group + g)],
            o_send.at[h, g],
            o_recv.at[h, g],
            device_id={"seq": other},
            device_id_type=MESH,
        )

    def keep_out(h, g):
        return pltpu.make_async_copy(
            keep.at[h, g], out.at[:, columns((parity * halves + h) * group + g)], o_keep.at[h, g]
        )

    def forward(h, back, side):
        if back > 0:

            @pl.when(pair >= back)
            def _():
                hop(h, back - 1, side).wait_recv()

        if back < depth:

            @pl.when((pair >= back) & (pair < last))
            def _():
                hop(h, back, side).start()

    small = [
        pltpu.make_async_copy(lengths_in, lengths, small_sem.at[0]),
        pltpu.make_async_copy(home_in, home, small_sem.at[1]),
    ]
    for h in range(halves):
        for t in range(2):
            load_kv(h, t).start()
    for copy in small:
        copy.start()
    for h in range(halves):
        for g in range(group):
            load_q(h, g).start()

    barrier = pltpu.get_barrier_semaphore()
    pl.semaphore_signal(barrier, inc=1, device_id={"seq": other}, device_id_type=MESH)

    @pl.when(pair > 0)
    def _():
        pl.semaphore_signal(barrier, inc=1, device_id={"seq": me - 2}, device_id_type=MESH)

    pl.semaphore_wait(barrier, 1 + (pair < last).astype(jnp.int32))

    for h in range(halves):
        for t in range(2):
            swap_kv(h, t).start()
    for h in range(halves):
        for t in range(2):
            load_kv(h, t).wait()
        forward(h, 0, parity)
    for h in range(halves):
        for g in range(group):
            swap_q(h, g).start()

    for copy in small:
        copy.wait()

    docs = lengths.shape[0]
    lane = lax.broadcasted_iota(jnp.int32, (8, HD), 1)

    def add_doc(doc, state):
        begin, starts, ends = state
        end = begin + lengths[doc]
        here = lane == doc
        return end, jnp.where(here, begin, starts), jnp.where(here, end, ends)

    nothing = jnp.zeros((8, HD), jnp.int32)
    _, starts, ends = lax.fori_loop(
        0, docs, add_doc, (jnp.int32(0), nothing, nothing), unroll=docs <= 16
    )
    starts, ends = starts[:1], ends[:1]
    offset = lax.broadcasted_iota(jnp.int32, (2 * rows, HD), 0)
    for back in range(depth + 1):
        position = (pair - back) * 2 * rows + offset
        inside = ((position >= starts) & (position < ends)) | (position < 0)
        kext[back] = jnp.where(inside, 1.0, 0.0).astype(kext.dtype)
        if back == 0:
            qext[...] = jnp.where(inside, 0.0, -FAR).astype(qext.dtype)
        else:

            @pl.when(pair < back)
            def _():
                for h in range(halves):
                    kv[h, :, back] = jnp.zeros(kv.shape[1:2] + kv.shape[3:], kv.dtype)

    mine = [(home[pair * blocks + b] == me).astype(jnp.int32) for b in range(blocks)]
    kept_at = [jnp.int32(0)] * per
    sent_at = [jnp.int32(0)] * per
    kept_count, sent_count = jnp.int32(0), jnp.int32(0)
    for b in range(blocks):
        for s in range(per):
            kept_at[s] = jnp.where((mine[b] == 1) & (kept_count == s), b, kept_at[s])
            sent_at[s] = jnp.where((mine[b] == 0) & (sent_count == s), b, sent_at[s])
        kept_count = kept_count + mine[b]
        sent_count = sent_count + 1 - mine[b]

    def take_swapped(h):
        for t in range(2):
            swap_kv(h, t).wait_recv()
        forward(h, 0, 1 - parity)

    def keys_of(h, t, back, low, high):
        found = []
        for side in range(2):
            begin, end = max(low - side * per, 0), min(high - side * per, per)
            if begin < end:
                at = pl.ds(begin * BLOCK, (end - begin) * BLOCK)
                found.append(kv[h, t, back, side, at])
        return jnp.concatenate(found, axis=0)

    def split(j, late):
        early, rest = [], []
        for back, low, high in spans(j, depth, blocks, reach):
            if late is None or back < depth:
                early.append((back, low, high))
                continue
            begin, end = max(low, late * per), min(high, (late + 1) * per)
            if begin < end:
                rest.append((back, begin, end))
            for begin, end in ((low, min(high, late * per)), (max(low, (late + 1) * per), high)):
                if begin < end:
                    early.append((back, begin, end))
        return early, rest

    def scored(h, first, j, runs):
        side, inner = j // per, j % per
        at = pl.ds(inner * BLOCK, BLOCK)
        block = jnp.concatenate([q[h, first + g, side, at] for g in range(chunk)], axis=0)
        extra = jnp.concatenate([qext[pl.ds(j * BLOCK, BLOCK)]] * chunk, axis=0)
        grouped = jnp.concatenate([block, extra], axis=1)
        seen = jnp.concatenate(
            [
                jnp.concatenate(
                    [keys_of(h, 0, back, low, high), kext[back, low * BLOCK : high * BLOCK]],
                    axis=1,
                )
                for back, low, high in runs
            ],
            axis=0,
        )
        raw = lax.dot_general(
            grouped, seen, (((1,), (1,)), ((), ())), preferred_element_type=jnp.float32
        )
        parts = []
        begin = 0
        for back, low, high in runs:
            for kb in range(low, high):
                part = raw[:, begin : begin + BLOCK]
                begin += BLOCK
                gap = (back * blocks + j - kb) * BLOCK
                row = lax.broadcasted_iota(jnp.int32, (BLOCK, BLOCK), 0)
                column = lax.broadcasted_iota(jnp.int32, (BLOCK, BLOCK), 1)
                allowed = None
                if gap < BLOCK:
                    allowed = gap + row >= column
                if windowed and gap + BLOCK > WINDOW:
                    allowed = gap + row - column < WINDOW
                if allowed is not None:
                    shaped = part.reshape(chunk, BLOCK, BLOCK)
                    part = jnp.where(allowed[None], shaped, -FAR).reshape(part.shape)
                parts.append(part)
        peak = parts[0]
        for part in parts[1:]:
            peak = jnp.maximum(peak, part)
        return parts, jnp.max(peak, axis=1, keepdims=True)

    def folded(h, parts, peak, runs):
        weights = jnp.concatenate(
            [jnp.exp2((part - peak) * scale).astype(jnp.bfloat16) for part in parts], axis=1
        )
        joined = jnp.concatenate(
            [keys_of(h, 1, back, low, high) for back, low, high in runs], axis=0
        )
        joined = jnp.concatenate([joined, jnp.ones_like(joined)], axis=1)
        return jnp.dot(weights, joined, preferred_element_type=jnp.float32)

    def finish(h, first, j, both):
        result = (both[:, :HD] / both[:, HD:]).astype(mixed.dtype)
        for g in range(chunk):
            mixed[h, first + g, j] = result[g * BLOCK : (g + 1) * BLOCK]

    def attend(h, step, late=None):
        for j in range(blocks):
            early, rest = split(j, late)
            parts, peak = scored(h, step * chunk, j, early)
            both = folded(h, parts, peak, early)
            if rest:
                top[step, j] = jnp.broadcast_to(peak, top.shape[2:])
                part_sum[step, j] = both
            else:
                finish(h, step * chunk, j, both)

    def complete(h, step, late):
        for j in range(blocks):
            _, rest = split(j, late)
            if rest:
                parts, peak = scored(h, step * chunk, j, rest)
                before = top[step, j]
                peak = jnp.maximum(before, peak)
                rescale = jnp.exp2((before - peak) * scale)
                both = folded(h, parts, peak, rest)
                both = both + part_sum[step, j] * jnp.concatenate([rescale, rescale], axis=1)
                finish(h, step * chunk, j, both)

    def deliver(h, first):
        for g in range(chunk):
            for s in range(per):
                give[h, first + g, pl.ds(s * BLOCK, BLOCK)] = mixed[h, first + g, sent_at[s]]
                keep[h, first + g, pl.ds(s * BLOCK, BLOCK)] = mixed[h, first + g, kept_at[s]]
            send_out(h, first + g).start()
            keep_out(h, first + g).start()

    def settle(h):
        for g in range(group):
            load_q(h, g).wait()
            swap_q(h, g).wait_recv()

    def arrive(h, backs, sides):
        for back in backs:
            for side in sides:
                forward(h, back, side)

    sides = (parity, 1 - parity)
    steps = group // chunk
    soon = range(1, 2 if depth > 1 else 1)
    take_swapped(0)
    arrive(0, soon, sides)
    for h in range(1, halves):
        take_swapped(h)
        arrive(h, soon, sides[:1])
    for h in range(halves):
        settle(h)
        later = range(soon.stop, depth + 1)
        if h + 1 < halves or depth == 0:
            arrive(h, later, sides)
            for step in range(steps):
                attend(h, step)
                deliver(h, step * chunk)
                if step == 0 and h + 1 < halves:
                    arrive(h + 1, soon, sides[1:])
            continue
        arrive(h, later[:-1], sides)
        arrive(h, later[-1:], sides[:1])

        @pl.loop(0, steps)
        def _(step):
            for side in range(2):

                @pl.when(parity == side)
                def _():
                    attend(h, step, 1 - side)

        arrive(h, later[-1:], sides[1:])

        @pl.loop(0, steps)
        def _(step):
            for side in range(2):

                @pl.when(parity == side)
                def _():
                    complete(h, step, 1 - side)

            deliver(h, step * chunk)

    for h in range(halves):
        for t in range(2):
            swap_kv(h, t).wait_send()
        for back in range(depth):
            for side in range(2):

                @pl.when((pair >= back) & (pair < last))
                def _():
                    hop(h, back, side).wait_send()

        for g in range(group):
            swap_q(h, g).wait_send()
            keep_out(h, g).wait()
            send_out(h, g).wait()


def local(queries, keys, values, lengths, home):
    rows, query_cols = queries.shape
    kv_heads = keys.shape[1] // HD
    group = query_cols // HD // kv_heads
    halves = kv_heads // 2
    blocks = 2 * rows // BLOCK
    seq = lax.axis_size("seq")
    tokens = seq * rows
    most_len = min(tokens // 2, 4096)
    reach = min(WINDOW, most_len)
    depth = min(-(-(reach - 1) // (2 * rows)), seq // 2 - 1)
    plan = (group, halves, depth, reach, most_len > WINDOW, 2)
    bf16 = jnp.bfloat16
    dma = pltpu.SemaphoreType.DMA
    anywhere = pl.BlockSpec(memory_space=pl.ANY)
    hbm = pl.BlockSpec(memory_space=pltpu.HBM)
    return pl.pallas_call(
        functools.partial(fused, plan),
        out_shape=pltpu.VMEM(queries.shape, bf16),
        in_specs=[hbm] * 5,
        out_specs=pl.BlockSpec(memory_space=pltpu.VMEM),
        scratch_shapes=[
            pltpu.SMEM(lengths.shape, jnp.int32),
            pltpu.SMEM(home.shape, jnp.int32),
            pltpu.VMEM((halves, group, 2, rows, HD), bf16),
            pltpu.VMEM((halves, 2, depth + 1, 2, rows, HD), bf16),
            pltpu.VMEM((2 * rows, HD), bf16),
            pltpu.VMEM((depth + 1, 2 * rows, HD), bf16),
            pltpu.VMEM((halves, group, blocks, BLOCK, HD), bf16),
            pltpu.VMEM((halves, group, rows, HD), bf16),
            pltpu.VMEM((halves, group, rows, HD), bf16),
            pltpu.VMEM((group // plan[-1], blocks, plan[-1] * BLOCK, HD), jnp.float32),
            pltpu.VMEM((group // plan[-1], blocks, plan[-1] * BLOCK, 2 * HD), jnp.float32),
            dma((2,)),
            dma((halves, 2)),
            dma((halves, group)),
            dma((halves, group)),
            dma((halves, group)),
            dma((halves, 2)),
            dma((halves, 2)),
            dma((halves, depth, 2)),
            dma((halves, depth, 2)),
            dma((halves, group)),
            dma((halves, group)),
            dma((halves, group)),
        ],
        compiler_params=pltpu.CompilerParams(
            collective_id=0, has_side_effects=True, vmem_limit_bytes=60 * 1024 * 1024
        ),
    )(lengths, home, queries, keys, values)


def solution(mesh):
    placed = (
        P(("pack", "seq"), None),
        P(("pack", "seq"), None),
        P(("pack", "seq"), None),
        P("pack"),
        P("pack"),
    )
    return jax.shard_map(
        local, mesh=mesh, in_specs=placed, out_specs=P(("pack", "seq"), None), check_vma=False
    )
```

```python
import functools

import jax
import jax.numpy as jnp
from jax import lax
from jax.experimental import pallas as pl
from jax.experimental.pallas import tpu as pltpu
from jax.sharding import PartitionSpec as P

HD = 128
BLOCK = 128
WINDOW = 2048
LOG2E = 1.4426950408889634
FAR = float(2**20)
MESH = pl.DeviceIdType.MESH


def spans(row_block, depth, blocks, reach):
    found = []
    for back in range(depth, -1, -1):
        near = [
            kb
            for kb in range(blocks)
            if -BLOCK < (back * blocks + row_block - kb) * BLOCK < reach + BLOCK - 1
        ]
        if near:
            found.append((back, near[0], near[-1] + 1))
    return found


def fused(
    plan, lengths_in, home_in, queries, keys, values, out,
    lengths, home, q, kv, qext, kext, mixed, give, keep, top, part_sum,
    small_sem, load_sem, q_load, q_send, q_recv, kv_send, kv_recv, hop_send, hop_recv, o_send, o_recv, o_keep,
):
    group, halves, depth, reach, windowed, chunk = plan
    rows = queries.shape[0]
    blocks = 2 * rows // BLOCK
    per = blocks // 2
    me = lax.axis_index("seq")
    count = lax.axis_size("seq")
    other = me ^ 1
    parity = me % 2
    pair = me // 2
    last = count // 2 - 1
    scale = HD ** (-0.5) * LOG2E

    def columns(head, wide=1):
        return pl.ds(pl.multiple_of(head * HD, HD), wide * HD)

    def load_kv(h, t):
        source = keys if t == 0 else values
        return pltpu.make_async_copy(
            source.at[:, columns(parity * halves + h)], kv.at[h, t, 0, parity], load_sem.at[h, t]
        )

    def load_q(h, g):
        return pltpu.make_async_copy(
            queries.at[:, columns((parity * halves + h) * group + g)],
            q.at[h, g, parity],
            q_load.at[h, g],
        )

    def swap_kv(h, t):
        source = keys if t == 0 else values
        return pltpu.make_async_remote_copy(
            source.at[:, columns((1 - parity) * halves + h)],
            kv.at[h, t, 0, parity],
            kv_send.at[h, t],
            kv_recv.at[h, t],
            device_id={"seq": other},
            device_id_type=MESH,
        )

    def swap_q(h, g):
        return pltpu.make_async_remote_copy(
            queries.at[:, columns(((1 - parity) * halves + h) * group + g)],
            q.at[h, g, parity],
            q_send.at[h, g],
            q_recv.at[h, g],
            device_id={"seq": other},
            device_id_type=MESH,
        )

    def hop(h, back, side):
        return pltpu.make_async_remote_copy(
            kv.at[h, :, back, side],
            kv.at[h, :, back + 1, side],
            hop_send.at[h, back, side],
            hop_recv.at[h, back, side],
            device_id={"seq": me + 2},
            device_id_type=MESH,
        )

    def send_out(h, g):
        return pltpu.make_async_remote_copy(
            give.at[h, g],
            out.at[:, columns((parity * halves + h) * group + g)],
            o_send.at[h, g],
            o_recv.at[h, g],
            device_id={"seq": other},
            device_id_type=MESH,
        )

    def keep_out(h, g):
        return pltpu.make_async_copy(
            keep.at[h, g], out.at[:, columns((parity * halves + h) * group + g)], o_keep.at[h, g]
        )

    def forward(h, back, side):
        if back > 0:

            @pl.when(pair >= back)
            def _():
                hop(h, back - 1, side).wait_recv()

        if back < depth:

            @pl.when((pair >= back) & (pair < last))
            def _():
                hop(h, back, side).start()

    small = [
        pltpu.make_async_copy(lengths_in, lengths, small_sem.at[0]),
        pltpu.make_async_copy(home_in, home, small_sem.at[1]),
    ]
    for h in range(halves):
        for t in range(2):
            load_kv(h, t).start()
    for copy in small:
        copy.start()
    for h in range(halves):
        for g in range(group):
            load_q(h, g).start()

    barrier = pltpu.get_barrier_semaphore()
    pl.semaphore_signal(barrier, inc=1, device_id={"seq": other}, device_id_type=MESH)

    @pl.when(pair > 0)
    def _():
        pl.semaphore_signal(barrier, inc=1, device_id={"seq": me - 2}, device_id_type=MESH)

    pl.semaphore_wait(barrier, 1 + (pair < last).astype(jnp.int32))

    for h in range(halves):
        for t in range(2):
            swap_kv(h, t).start()
    for h in range(halves):
        for t in range(2):
            load_kv(h, t).wait()
        forward(h, 0, parity)
    for h in range(halves):
        for g in range(group):
            swap_q(h, g).start()

    for copy in small:
        copy.wait()

    docs = lengths.shape[0]
    lane = lax.broadcasted_iota(jnp.int32, (8, HD), 1)

    def add_doc(doc, state):
        begin, starts, ends = state
        end = begin + lengths[doc]
        here = lane == doc
        return end, jnp.where(here, begin, starts), jnp.where(here, end, ends)

    nothing = jnp.zeros((8, HD), jnp.int32)
    _, starts, ends = lax.fori_loop(
        0, docs, add_doc, (jnp.int32(0), nothing, nothing), unroll=docs <= 16
    )
    starts, ends = starts[:1], ends[:1]
    offset = lax.broadcasted_iota(jnp.int32, (2 * rows, HD), 0)
    for back in range(depth + 1):
        position = (pair - back) * 2 * rows + offset
        inside = ((position >= starts) & (position < ends)) | (position < 0)
        kext[back] = jnp.where(inside, 1.0, 0.0).astype(kext.dtype)
        if back == 0:
            qext[...] = jnp.where(inside, 0.0, -FAR).astype(qext.dtype)
        else:

            @pl.when(pair < back)
            def _():
                for h in range(halves):
                    kv[h, :, back] = jnp.zeros(kv.shape[1:2] + kv.shape[3:], kv.dtype)

    mine = [(home[pair * blocks + b] == me).astype(jnp.int32) for b in range(blocks)]
    kept_at = [jnp.int32(0)] * per
    sent_at = [jnp.int32(0)] * per
    kept_count, sent_count = jnp.int32(0), jnp.int32(0)
    for b in range(blocks):
        for s in range(per):
            kept_at[s] = jnp.where((mine[b] == 1) & (kept_count == s), b, kept_at[s])
            sent_at[s] = jnp.where((mine[b] == 0) & (sent_count == s), b, sent_at[s])
        kept_count = kept_count + mine[b]
        sent_count = sent_count + 1 - mine[b]

    def take_swapped(h):
        for t in range(2):
            swap_kv(h, t).wait_recv()
        forward(h, 0, 1 - parity)

    def keys_of(h, t, back, low, high):
        found = []
        for side in range(2):
            begin, end = max(low - side * per, 0), min(high - side * per, per)
            if begin < end:
                at = pl.ds(begin * BLOCK, (end - begin) * BLOCK)
                found.append(kv[h, t, back, side, at])
        return jnp.concatenate(found, axis=0)

    def stages(j, own):
        found = [[], [], []]
        for back, low, high in spans(j, depth, blocks, reach):
            if back < depth or depth == 0:
                found[0].append((back, low, high))
                continue
            for stage, side in ((1, own), (2, 1 - own)):
                begin, end = max(low, side * per), min(high, (side + 1) * per)
                if begin < end:
                    found[stage].append((back, begin, end))
        return found

    def scored(h, first, j, runs):
        side, inner = j // per, j % per
        at = pl.ds(inner * BLOCK, BLOCK)
        block = jnp.concatenate([q[h, first + g, side, at] for g in range(chunk)], axis=0)
        extra = jnp.concatenate([qext[pl.ds(j * BLOCK, BLOCK)]] * chunk, axis=0)
        grouped = jnp.concatenate([block, extra], axis=1)
        seen = jnp.concatenate(
            [
                jnp.concatenate(
                    [keys_of(h, 0, back, low, high), kext[back, low * BLOCK : high * BLOCK]],
                    axis=1,
                )
                for back, low, high in runs
            ],
            axis=0,
        )
        raw = lax.dot_general(
            grouped, seen, (((1,), (1,)), ((), ())), preferred_element_type=jnp.float32
        )
        parts = []
        begin = 0
        for back, low, high in runs:
            for kb in range(low, high):
                part = raw[:, begin : begin + BLOCK]
                begin += BLOCK
                gap = (back * blocks + j - kb) * BLOCK
                row = lax.broadcasted_iota(jnp.int32, (BLOCK, BLOCK), 0)
                column = lax.broadcasted_iota(jnp.int32, (BLOCK, BLOCK), 1)
                allowed = None
                if gap < BLOCK:
                    allowed = gap + row >= column
                if windowed and gap + BLOCK > WINDOW:
                    allowed = gap + row - column < WINDOW
                if allowed is not None:
                    shaped = part.reshape(chunk, BLOCK, BLOCK)
                    part = jnp.where(allowed[None], shaped, -FAR).reshape(part.shape)
                parts.append(part)
        peak = parts[0]
        for part in parts[1:]:
            peak = jnp.maximum(peak, part)
        return parts, jnp.max(peak, axis=1, keepdims=True)

    def folded(h, parts, peak, runs):
        weights = jnp.concatenate(
            [jnp.exp2((part - peak) * scale).astype(jnp.bfloat16) for part in parts], axis=1
        )
        joined = jnp.concatenate(
            [keys_of(h, 1, back, low, high) for back, low, high in runs], axis=0
        )
        joined = jnp.concatenate([joined, jnp.ones_like(joined)], axis=1)
        return jnp.dot(weights, joined, preferred_element_type=jnp.float32)

    def finish(h, first, j, both):
        result = (both[:, :HD] / both[:, HD:]).astype(mixed.dtype)
        for g in range(chunk):
            mixed[h, first + g, j] = result[g * BLOCK : (g + 1) * BLOCK]

    def attend(h, step, own, begin, end):
        for j in range(blocks):
            found = stages(j, own)
            runs = sum(found[begin:end], [])
            if not runs:
                continue
            parts, peak = scored(h, step * chunk, j, runs)
            if begin > 0:
                before = top[step, j]
                peak = jnp.maximum(before, peak)
                rescale = jnp.exp2((before - peak) * scale)
            both = folded(h, parts, peak, runs)
            if begin > 0:
                both = both + part_sum[step, j] * jnp.concatenate([rescale, rescale], axis=1)
            if any(found[end:]):
                top[step, j] = jnp.broadcast_to(peak, top.shape[2:])
                part_sum[step, j] = both
            else:
                finish(h, step * chunk, j, both)

    def by_parity(h, step, begin, end):
        for side in range(2):

            @pl.when(parity == side)
            def _():
                attend(h, step, side, begin, end)

    def deliver(h, first):
        for g in range(chunk):
            for s in range(per):
                give[h, first + g, pl.ds(s * BLOCK, BLOCK)] = mixed[h, first + g, sent_at[s]]
                keep[h, first + g, pl.ds(s * BLOCK, BLOCK)] = mixed[h, first + g, kept_at[s]]
            send_out(h, first + g).start()
            keep_out(h, first + g).start()

    def settle(h, step):
        for g in range(chunk):
            load_q(h, step * chunk + g).wait()
            swap_q(h, step * chunk + g).wait_recv()

    def arrive(h, backs, sides):
        for back in backs:
            for side in sides:
                forward(h, back, side)

    sides = (parity, 1 - parity)
    steps = group // chunk
    soon = range(1, 2 if depth > 1 else 1)
    take_swapped(0)
    arrive(0, soon, sides)
    for h in range(1, halves):
        take_swapped(h)
        arrive(h, soon, sides[:1])
    later = range(soon.stop, depth + 1)
    for h in range(halves):
        if h > 0:
            arrive(h, soon, sides[1:])
        arrive(h, later[:-1], sides)
        joined = 2 if h == 0 else 1
        if joined == 2:
            arrive(h, later[-1:], sides[:1])

        @pl.loop(0, steps)
        def _(step):
            settle(h, step)
            if joined == 2:
                by_parity(h, step, 0, 2)
            else:
                attend(h, step, 0, 0, 1)

        if joined == 1:
            arrive(h, later[-1:], sides[:1])

            @pl.loop(0, steps)
            def _(step):
                by_parity(h, step, 1, 2)

        arrive(h, later[-1:], sides[1:])

        @pl.loop(0, steps)
        def _(step):
            by_parity(h, step, 2, 3)
            deliver(h, step * chunk)

    for h in range(halves):
        for t in range(2):
            swap_kv(h, t).wait_send()
        for back in range(depth):
            for side in range(2):

                @pl.when((pair >= back) & (pair < last))
                def _():
                    hop(h, back, side).wait_send()

        for g in range(group):
            swap_q(h, g).wait_send()
            keep_out(h, g).wait()
            send_out(h, g).wait()


def local(queries, keys, values, lengths, home):
    rows, query_cols = queries.shape
    kv_heads = keys.shape[1] // HD
    group = query_cols // HD // kv_heads
    halves = kv_heads // 2
    blocks = 2 * rows // BLOCK
    seq = lax.axis_size("seq")
    tokens = seq * rows
    most_len = min(tokens // 2, 4096)
    reach = min(WINDOW, most_len)
    depth = min(-(-(reach - 1) // (2 * rows)), seq // 2 - 1)
    plan = (group, halves, depth, reach, most_len > WINDOW, 2)
    bf16 = jnp.bfloat16
    dma = pltpu.SemaphoreType.DMA
    anywhere = pl.BlockSpec(memory_space=pl.ANY)
    hbm = pl.BlockSpec(memory_space=pltpu.HBM)
    return pl.pallas_call(
        functools.partial(fused, plan),
        out_shape=pltpu.VMEM(queries.shape, bf16),
        in_specs=[hbm] * 5,
        out_specs=pl.BlockSpec(memory_space=pltpu.VMEM),
        scratch_shapes=[
            pltpu.SMEM(lengths.shape, jnp.int32),
            pltpu.SMEM(home.shape, jnp.int32),
            pltpu.VMEM((halves, group, 2, rows, HD), bf16),
            pltpu.VMEM((halves, 2, depth + 1, 2, rows, HD), bf16),
            pltpu.VMEM((2 * rows, HD), bf16),
            pltpu.VMEM((depth + 1, 2 * rows, HD), bf16),
            pltpu.VMEM((halves, group, blocks, BLOCK, HD), bf16),
            pltpu.VMEM((halves, group, rows, HD), bf16),
            pltpu.VMEM((halves, group, rows, HD), bf16),
            pltpu.VMEM((group // plan[-1], blocks, plan[-1] * BLOCK, HD), jnp.float32),
            pltpu.VMEM((group // plan[-1], blocks, plan[-1] * BLOCK, 2 * HD), jnp.float32),
            dma((2,)),
            dma((halves, 2)),
            dma((halves, group)),
            dma((halves, group)),
            dma((halves, group)),
            dma((halves, 2)),
            dma((halves, 2)),
            dma((halves, depth, 2)),
            dma((halves, depth, 2)),
            dma((halves, group)),
            dma((halves, group)),
            dma((halves, group)),
        ],
        compiler_params=pltpu.CompilerParams(
            collective_id=0, has_side_effects=True, vmem_limit_bytes=60 * 1024 * 1024
        ),
    )(lengths, home, queries, keys, values)


def solution(mesh):
    placed = (
        P(("pack", "seq"), None),
        P(("pack", "seq"), None),
        P(("pack", "seq"), None),
        P("pack"),
        P("pack"),
    )
    return jax.shard_map(
        local, mesh=mesh, in_specs=placed, out_specs=P(("pack", "seq"), None), check_vma=False
    )
```

```python
import functools

import jax
import jax.numpy as jnp
from jax import lax
from jax.experimental import pallas as pl
from jax.experimental.pallas import tpu as pltpu
from jax.sharding import PartitionSpec as P

HD = 128
BLOCK = 128
WINDOW = 2048
LOG2E = 1.4426950408889634
FAR = float(2**20)
MESH = pl.DeviceIdType.MESH


def spans(row_block, depth, blocks, reach):
    found = []
    for back in range(depth, -1, -1):
        near = [
            kb
            for kb in range(blocks)
            if -BLOCK < (back * blocks + row_block - kb) * BLOCK < reach + BLOCK - 1
        ]
        if near:
            found.append((back, near[0], near[-1] + 1))
    return found


def fused(
    plan, lengths_in, home_in, queries, keys, values, out,
    lengths, home, q, kv, qext, kext, mixed, give, keep, top, part_sum,
    ready, small_sem, load_sem, q_load, q_send, q_recv, kv_send, kv_recv, hop_send, hop_recv, o_send, o_recv, o_keep,
):
    group, halves, depth, reach, windowed, chunk = plan
    rows = queries.shape[0]
    blocks = 2 * rows // BLOCK
    per = blocks // 2
    me = lax.axis_index("seq")
    count = lax.axis_size("seq")
    other = me ^ 1
    parity = me % 2
    pair = me // 2
    last = count // 2 - 1
    scale = HD ** (-0.5) * LOG2E

    def columns(head, wide=1):
        return pl.ds(pl.multiple_of(head * HD, HD), wide * HD)

    def load_kv(h, t):
        source = keys if t == 0 else values
        return pltpu.make_async_copy(
            source.at[:, columns(parity * halves + h)], kv.at[h, t, 0, parity], load_sem.at[h, t]
        )

    def load_q(h, g):
        return pltpu.make_async_copy(
            queries.at[:, columns((parity * halves + h) * group + g)],
            q.at[h, g, parity],
            q_load.at[h, g],
        )

    def swap_kv(h, t):
        source = keys if t == 0 else values
        return pltpu.make_async_remote_copy(
            source.at[:, columns((1 - parity) * halves + h)],
            kv.at[h, t, 0, parity],
            kv_send.at[h, t],
            kv_recv.at[h, t],
            device_id={"seq": other},
            device_id_type=MESH,
        )

    def swap_q(h, g):
        return pltpu.make_async_remote_copy(
            queries.at[:, columns(((1 - parity) * halves + h) * group + g)],
            q.at[h, g, parity],
            q_send.at[h, g],
            q_recv.at[h, g],
            device_id={"seq": other},
            device_id_type=MESH,
        )

    def hop(h, back, side):
        return pltpu.make_async_remote_copy(
            kv.at[h, :, back, side],
            kv.at[h, :, back + 1, side],
            hop_send.at[h, back, side],
            hop_recv.at[h, back, side],
            device_id={"seq": me + 2},
            device_id_type=MESH,
        )

    def send_out(h, g):
        return pltpu.make_async_remote_copy(
            give.at[h, g],
            out.at[:, columns((parity * halves + h) * group + g)],
            o_send.at[h, g],
            o_recv.at[h, g],
            device_id={"seq": other},
            device_id_type=MESH,
        )

    def keep_out(h, g):
        return pltpu.make_async_copy(
            keep.at[h, g], out.at[:, columns((parity * halves + h) * group + g)], o_keep.at[h, g]
        )

    def forward(h, back, side):
        if back > 0:

            @pl.when(pair >= back)
            def _():
                hop(h, back - 1, side).wait_recv()

        if back < depth:

            @pl.when((pair >= back) & (pair < last))
            def _():
                hop(h, back, side).start()

    small = [
        pltpu.make_async_copy(lengths_in, lengths, small_sem.at[0]),
        pltpu.make_async_copy(home_in, home, small_sem.at[1]),
    ]
    for h in range(halves):
        for t in range(2):
            load_kv(h, t).start()
    for copy in small:
        copy.start()
    for h in range(halves):
        for g in range(group):
            load_q(h, g).start()

    barrier = pltpu.get_barrier_semaphore()
    pl.semaphore_signal(barrier, inc=1, device_id={"seq": other}, device_id_type=MESH)

    @pl.when((parity == 0) & (pair > 0))
    def _():
        pl.semaphore_signal(barrier, inc=1, device_id={"seq": me - 2}, device_id_type=MESH)

    @pl.when((parity == 1) & (pair < last))
    def _():
        pl.semaphore_signal(barrier, inc=1, device_id={"seq": me + 2}, device_id_type=MESH)

    greeted = jnp.where(parity == 0, pair < last, pair > 0)
    pl.semaphore_wait(barrier, 1 + greeted.astype(jnp.int32))

    @pl.when((parity == 1) & (pair > 0))
    def _():
        pl.semaphore_signal(ready, inc=1, device_id={"seq": me - 2}, device_id_type=MESH)

    for h in range(halves):
        for t in range(2):
            swap_kv(h, t).start()

    @pl.when((parity == 1) & (pair < last))
    def _():
        pl.semaphore_wait(ready, 1)

    for h in range(halves):
        for t in range(2):
            load_kv(h, t).wait()
        forward(h, 0, parity)
    for h in range(halves):
        for g in range(group):
            swap_q(h, g).start()

    for copy in small:
        copy.wait()

    docs = lengths.shape[0]
    lane = lax.broadcasted_iota(jnp.int32, (8, HD), 1)

    def add_doc(doc, state):
        begin, starts, ends = state
        end = begin + lengths[doc]
        here = lane == doc
        return end, jnp.where(here, begin, starts), jnp.where(here, end, ends)

    nothing = jnp.zeros((8, HD), jnp.int32)
    _, starts, ends = lax.fori_loop(
        0, docs, add_doc, (jnp.int32(0), nothing, nothing), unroll=docs <= 16
    )
    starts, ends = starts[:1], ends[:1]
    offset = lax.broadcasted_iota(jnp.int32, (2 * rows, HD), 0)
    for back in range(depth + 1):
        position = (pair - back) * 2 * rows + offset
        inside = ((position >= starts) & (position < ends)) | (position < 0)
        kext[back] = jnp.where(inside, 1.0, 0.0).astype(kext.dtype)
        if back == 0:
            qext[...] = jnp.where(inside, 0.0, -FAR).astype(qext.dtype)
        else:

            @pl.when(pair < back)
            def _():
                for h in range(halves):
                    kv[h, :, back] = jnp.zeros(kv.shape[1:2] + kv.shape[3:], kv.dtype)

    mine = [(home[pair * blocks + b] == me).astype(jnp.int32) for b in range(blocks)]
    kept_at = [jnp.int32(0)] * per
    sent_at = [jnp.int32(0)] * per
    kept_count, sent_count = jnp.int32(0), jnp.int32(0)
    for b in range(blocks):
        for s in range(per):
            kept_at[s] = jnp.where((mine[b] == 1) & (kept_count == s), b, kept_at[s])
            sent_at[s] = jnp.where((mine[b] == 0) & (sent_count == s), b, sent_at[s])
        kept_count = kept_count + mine[b]
        sent_count = sent_count + 1 - mine[b]

    def take_swapped(h):
        for t in range(2):
            swap_kv(h, t).wait_recv()
        forward(h, 0, 1 - parity)

    def keys_of(h, t, back, low, high):
        found = []
        for side in range(2):
            begin, end = max(low - side * per, 0), min(high - side * per, per)
            if begin < end:
                at = pl.ds(begin * BLOCK, (end - begin) * BLOCK)
                found.append(kv[h, t, back, side, at])
        return jnp.concatenate(found, axis=0)

    def stages(j, own):
        found = [[], [], []]
        for back, low, high in spans(j, depth, blocks, reach):
            if back < depth or depth == 0:
                found[0].append((back, low, high))
                continue
            for stage, side in ((1, own), (2, 1 - own)):
                begin, end = max(low, side * per), min(high, (side + 1) * per)
                if begin < end:
                    found[stage].append((back, begin, end))
        return found

    def scored(h, first, j, runs):
        side, inner = j // per, j % per
        at = pl.ds(inner * BLOCK, BLOCK)
        block = jnp.concatenate([q[h, first + g, side, at] for g in range(chunk)], axis=0)
        extra = jnp.concatenate([qext[pl.ds(j * BLOCK, BLOCK)]] * chunk, axis=0)
        grouped = jnp.concatenate([block, extra], axis=1)
        seen = jnp.concatenate(
            [
                jnp.concatenate(
                    [keys_of(h, 0, back, low, high), kext[back, low * BLOCK : high * BLOCK]],
                    axis=1,
                )
                for back, low, high in runs
            ],
            axis=0,
        )
        raw = lax.dot_general(
            grouped, seen, (((1,), (1,)), ((), ())), preferred_element_type=jnp.float32
        )
        parts = []
        begin = 0
        for back, low, high in runs:
            for kb in range(low, high):
                part = raw[:, begin : begin + BLOCK]
                begin += BLOCK
                gap = (back * blocks + j - kb) * BLOCK
                row = lax.broadcasted_iota(jnp.int32, (BLOCK, BLOCK), 0)
                column = lax.broadcasted_iota(jnp.int32, (BLOCK, BLOCK), 1)
                allowed = None
                if gap < BLOCK:
                    allowed = gap + row >= column
                if windowed and gap + BLOCK > WINDOW:
                    allowed = gap + row - column < WINDOW
                if allowed is not None:
                    shaped = part.reshape(chunk, BLOCK, BLOCK)
                    part = jnp.where(allowed[None], shaped, -FAR).reshape(part.shape)
                parts.append(part)
        peak = parts[0]
        for part in parts[1:]:
            peak = jnp.maximum(peak, part)
        return parts, jnp.max(peak, axis=1, keepdims=True)

    def folded(h, parts, peak, runs):
        weights = jnp.concatenate(
            [jnp.exp2((part - peak) * scale).astype(jnp.bfloat16) for part in parts], axis=1
        )
        joined = jnp.concatenate(
            [keys_of(h, 1, back, low, high) for back, low, high in runs], axis=0
        )
        joined = jnp.concatenate([joined, jnp.ones_like(joined)], axis=1)
        return jnp.dot(weights, joined, preferred_element_type=jnp.float32)

    def finish(h, first, j, both):
        result = (both[:, :HD] / both[:, HD:]).astype(mixed.dtype)
        for g in range(chunk):
            mixed[h, first + g, j] = result[g * BLOCK : (g + 1) * BLOCK]

    def attend(h, step, own, begin, end):
        for j in range(blocks):
            found = stages(j, own)
            runs = sum(found[begin:end], [])
            if not runs:
                continue
            parts, peak = scored(h, step * chunk, j, runs)
            if begin > 0:
                before = top[step, j]
                peak = jnp.maximum(before, peak)
                rescale = jnp.exp2((before - peak) * scale)
            both = folded(h, parts, peak, runs)
            if begin > 0:
                both = both + part_sum[step, j] * jnp.concatenate([rescale, rescale], axis=1)
            if any(found[end:]):
                top[step, j] = jnp.broadcast_to(peak, top.shape[2:])
                part_sum[step, j] = both
            else:
                finish(h, step * chunk, j, both)

    def by_parity(h, step, begin, end):
        for side in range(2):

            @pl.when(parity == side)
            def _():
                attend(h, step, side, begin, end)

    def deliver(h, first):
        for g in range(chunk):
            for s in range(per):
                give[h, first + g, pl.ds(s * BLOCK, BLOCK)] = mixed[h, first + g, sent_at[s]]
                keep[h, first + g, pl.ds(s * BLOCK, BLOCK)] = mixed[h, first + g, kept_at[s]]
            send_out(h, first + g).start()
            keep_out(h, first + g).start()

    def settle(h, step):
        for g in range(chunk):
            load_q(h, step * chunk + g).wait()
            swap_q(h, step * chunk + g).wait_recv()

    def arrive(h, backs, sides):
        for back in backs:
            for side in sides:
                forward(h, back, side)

    sides = (parity, 1 - parity)
    steps = group // chunk
    soon = range(1, 2 if depth > 1 else 1)
    take_swapped(0)
    arrive(0, soon, sides)
    for h in range(1, halves):
        take_swapped(h)
        arrive(h, soon, sides[:1])
    later = range(soon.stop, depth + 1)
    for h in range(halves):
        if h > 0:
            arrive(h, soon, sides[1:])
        arrive(h, later[:-1], sides)
        joined = 2 if h == 0 else 1
        if joined == 2:
            arrive(h, later[-1:], sides[:1])

        @pl.loop(0, steps)
        def _(step):
            settle(h, step)
            if joined == 2:
                by_parity(h, step, 0, 2)
            else:
                attend(h, step, 0, 0, 1)

        if joined == 1:
            arrive(h, later[-1:], sides[:1])

            @pl.loop(0, steps)
            def _(step):
                by_parity(h, step, 1, 2)

        arrive(h, later[-1:], sides[1:])

        @pl.loop(0, steps)
        def _(step):
            by_parity(h, step, 2, 3)
            deliver(h, step * chunk)

    for h in range(halves):
        for t in range(2):
            swap_kv(h, t).wait_send()
        for back in range(depth):
            for side in range(2):

                @pl.when((pair >= back) & (pair < last))
                def _():
                    hop(h, back, side).wait_send()

        for g in range(group):
            swap_q(h, g).wait_send()
            keep_out(h, g).wait()
            send_out(h, g).wait()


def local(queries, keys, values, lengths, home):
    rows, query_cols = queries.shape
    kv_heads = keys.shape[1] // HD
    group = query_cols // HD // kv_heads
    halves = kv_heads // 2
    blocks = 2 * rows // BLOCK
    seq = lax.axis_size("seq")
    tokens = seq * rows
    most_len = min(tokens // 2, 4096)
    reach = min(WINDOW, most_len)
    depth = min(-(-(reach - 1) // (2 * rows)), seq // 2 - 1)
    plan = (group, halves, depth, reach, most_len > WINDOW, 2)
    bf16 = jnp.bfloat16
    dma = pltpu.SemaphoreType.DMA
    anywhere = pl.BlockSpec(memory_space=pl.ANY)
    hbm = pl.BlockSpec(memory_space=pltpu.HBM)
    return pl.pallas_call(
        functools.partial(fused, plan),
        out_shape=pltpu.VMEM(queries.shape, bf16),
        in_specs=[hbm] * 5,
        out_specs=pl.BlockSpec(memory_space=pltpu.VMEM),
        scratch_shapes=[
            pltpu.SMEM(lengths.shape, jnp.int32),
            pltpu.SMEM(home.shape, jnp.int32),
            pltpu.VMEM((halves, group, 2, rows, HD), bf16),
            pltpu.VMEM((halves, 2, depth + 1, 2, rows, HD), bf16),
            pltpu.VMEM((2 * rows, HD), bf16),
            pltpu.VMEM((depth + 1, 2 * rows, HD), bf16),
            pltpu.VMEM((halves, group, blocks, BLOCK, HD), bf16),
            pltpu.VMEM((halves, group, rows, HD), bf16),
            pltpu.VMEM((halves, group, rows, HD), bf16),
            pltpu.VMEM((group // plan[-1], blocks, plan[-1] * BLOCK, HD), jnp.float32),
            pltpu.VMEM((group // plan[-1], blocks, plan[-1] * BLOCK, 2 * HD), jnp.float32),
            pltpu.SemaphoreType.REGULAR,
            dma((2,)),
            dma((halves, 2)),
            dma((halves, group)),
            dma((halves, group)),
            dma((halves, group)),
            dma((halves, 2)),
            dma((halves, 2)),
            dma((halves, depth, 2)),
            dma((halves, depth, 2)),
            dma((halves, group)),
            dma((halves, group)),
            dma((halves, group)),
        ],
        compiler_params=pltpu.CompilerParams(
            collective_id=0, has_side_effects=True, vmem_limit_bytes=60 * 1024 * 1024
        ),
    )(lengths, home, queries, keys, values)


def solution(mesh):
    placed = (
        P(("pack", "seq"), None),
        P(("pack", "seq"), None),
        P(("pack", "seq"), None),
        P("pack"),
        P("pack"),
    )
    return jax.shard_map(
        local, mesh=mesh, in_specs=placed, out_specs=P(("pack", "seq"), None), check_vma=False
    )
```

```python
import functools

import jax
import jax.numpy as jnp
from jax import lax
from jax.experimental import pallas as pl
from jax.experimental.pallas import tpu as pltpu
from jax.sharding import PartitionSpec as P

HD = 128
BLOCK = 128
WINDOW = 2048
LOG2E = 1.4426950408889634
FAR = float(2**20)
MESH = pl.DeviceIdType.MESH


def spans(row_block, depth, blocks, reach):
    found = []
    for back in range(depth, -1, -1):
        near = [
            kb
            for kb in range(blocks)
            if -BLOCK < (back * blocks + row_block - kb) * BLOCK < reach + BLOCK - 1
        ]
        if near:
            found.append((back, near[0], near[-1] + 1))
    return found


def fused(
    plan, lengths_in, home_in, queries, keys, values, out,
    lengths, home, q, kv, qext, kext, mixed, give, keep, top, part_sum,
    ready, small_sem, load_sem, q_load, q_send, q_recv, kv_send, kv_recv, hop_send, hop_recv, o_send, o_recv, o_keep,
):
    group, halves, depth, reach, windowed, chunk = plan
    rows = queries.shape[0]
    blocks = 2 * rows // BLOCK
    per = blocks // 2
    me = lax.axis_index("seq")
    count = lax.axis_size("seq")
    other = me ^ 1
    parity = me % 2
    pair = me // 2
    last = count // 2 - 1
    scale = HD ** (-0.5) * LOG2E
    far = [j for j in range(blocks) if (depth, 0) in [run[:2] for run in spans(j, depth, blocks, reach)]]
    split = depth > 0 and per > 1 and far == [0]

    def columns(head, wide=1):
        return pl.ds(pl.multiple_of(head * HD, HD), wide * HD)

    def load_kv(h, t):
        source = keys if t == 0 else values
        return pltpu.make_async_copy(
            source.at[:, columns(parity * halves + h)], kv.at[h, t, 0, parity], load_sem.at[h, t]
        )

    def load_q(h, g):
        return pltpu.make_async_copy(
            queries.at[:, columns((parity * halves + h) * group + g)],
            q.at[h, g, parity],
            q_load.at[h, g],
        )

    def swap_kv(h, t):
        source = keys if t == 0 else values
        return pltpu.make_async_remote_copy(
            source.at[:, columns((1 - parity) * halves + h)],
            kv.at[h, t, 0, parity],
            kv_send.at[h, t],
            kv_recv.at[h, t],
            device_id={"seq": other},
            device_id_type=MESH,
        )

    def swap_q(h, g):
        return pltpu.make_async_remote_copy(
            queries.at[:, columns(((1 - parity) * halves + h) * group + g)],
            q.at[h, g, parity],
            q_send.at[h, g],
            q_recv.at[h, g],
            device_id={"seq": other},
            device_id_type=MESH,
        )

    def is_split(h, back, side):
        return split and h == halves - 1 and back == depth - 1 and side == 0

    def hop_rows(h, back, side, begin, end, part):
        return pltpu.make_async_remote_copy(
            kv.at[h, :, back, side, pl.ds(begin, end - begin)],
            kv.at[h, :, back + 1, side, pl.ds(begin, end - begin)],
            hop_send.at[h, back, side, part],
            hop_recv.at[h, back, side, part],
            device_id={"seq": me + 2},
            device_id_type=MESH,
        )

    def last_hop():
        return hop_rows(halves - 1, depth - 1, 0, 0, BLOCK, 1)

    def each_hop(h, back, side, act):
        if not (split and h == halves - 1 and back == depth - 1):
            act(hop_rows(h, back, side, 0, rows, 0))
            return
        for fixed in range(2):

            @pl.when(side == fixed)
            def _():
                act(hop_rows(h, back, fixed, BLOCK if is_split(h, back, fixed) else 0, rows, 0))

    def out_part(h, g, slots):
        at = pl.ds(slots[0] * BLOCK, len(slots) * BLOCK)
        return at, out.at[at, columns((parity * halves + h) * group + g)]

    def send_out(h, g, slots):
        at, place = out_part(h, g, slots)
        return pltpu.make_async_remote_copy(
            give.at[h, g, at],
            place,
            o_send.at[h, g, slots[0]],
            o_recv.at[h, g, slots[0]],
            device_id={"seq": other},
            device_id_type=MESH,
        )

    def keep_out(h, g, slots):
        at, place = out_part(h, g, slots)
        return pltpu.make_async_copy(keep.at[h, g, at], place, o_keep.at[h, g, slots[0]])

    def batches(h):
        if split and h == halves - 1:
            return [list(range(1, per)), [0]]
        return [list(range(per))]

    def forward(h, back, side):
        if back > 0:

            @pl.when(pair >= back)
            def _():
                each_hop(h, back - 1, side, lambda copy: copy.wait_recv())

        if back < depth:

            @pl.when((pair >= back) & (pair < last))
            def _():
                each_hop(h, back, side, lambda copy: copy.start())

    small = [
        pltpu.make_async_copy(lengths_in, lengths, small_sem.at[0]),
        pltpu.make_async_copy(home_in, home, small_sem.at[1]),
    ]
    for h in range(halves):
        for t in range(2):
            load_kv(h, t).start()
    for copy in small:
        copy.start()
    for h in range(halves):
        for g in range(group):
            load_q(h, g).start()

    barrier = pltpu.get_barrier_semaphore()
    pl.semaphore_signal(barrier, inc=1, device_id={"seq": other}, device_id_type=MESH)

    @pl.when((parity == 0) & (pair > 0))
    def _():
        pl.semaphore_signal(barrier, inc=1, device_id={"seq": me - 2}, device_id_type=MESH)

    @pl.when((parity == 1) & (pair < last))
    def _():
        pl.semaphore_signal(barrier, inc=1, device_id={"seq": me + 2}, device_id_type=MESH)

    greeted = jnp.where(parity == 0, pair < last, pair > 0)
    pl.semaphore_wait(barrier, 1 + greeted.astype(jnp.int32))

    @pl.when((parity == 1) & (pair > 0))
    def _():
        pl.semaphore_signal(ready, inc=1, device_id={"seq": me - 2}, device_id_type=MESH)

    for h in range(halves):
        for t in range(2):
            swap_kv(h, t).start()

    @pl.when((parity == 1) & (pair < last))
    def _():
        pl.semaphore_wait(ready, 1)

    for h in range(halves):
        for t in range(2):
            load_kv(h, t).wait()
        forward(h, 0, parity)
    for h in range(halves):
        for g in range(group):
            swap_q(h, g).start()

    for copy in small:
        copy.wait()

    docs = lengths.shape[0]
    lane = lax.broadcasted_iota(jnp.int32, (8, HD), 1)

    def add_doc(doc, state):
        begin, starts, ends = state
        end = begin + lengths[doc]
        here = lane == doc
        return end, jnp.where(here, begin, starts), jnp.where(here, end, ends)

    nothing = jnp.zeros((8, HD), jnp.int32)
    _, starts, ends = lax.fori_loop(
        0, docs, add_doc, (jnp.int32(0), nothing, nothing), unroll=docs <= 16
    )
    starts, ends = starts[:1], ends[:1]
    offset = lax.broadcasted_iota(jnp.int32, (2 * rows, HD), 0)
    for back in range(depth + 1):
        position = (pair - back) * 2 * rows + offset
        inside = ((position >= starts) & (position < ends)) | (position < 0)
        kext[back] = jnp.where(inside, 1.0, 0.0).astype(kext.dtype)
        if back == 0:
            qext[...] = jnp.where(inside, 0.0, -FAR).astype(qext.dtype)
        else:

            @pl.when(pair < back)
            def _():
                for h in range(halves):
                    kv[h, :, back] = jnp.zeros(kv.shape[1:2] + kv.shape[3:], kv.dtype)

    mine = [(home[pair * blocks + b] == me).astype(jnp.int32) for b in range(blocks)]
    kept_at = [jnp.int32(0)] * per
    sent_at = [jnp.int32(0)] * per
    kept_count, sent_count = jnp.int32(0), jnp.int32(0)
    for b in range(blocks):
        for s in range(per):
            kept_at[s] = jnp.where((mine[b] == 1) & (kept_count == s), b, kept_at[s])
            sent_at[s] = jnp.where((mine[b] == 0) & (sent_count == s), b, sent_at[s])
        kept_count = kept_count + mine[b]
        sent_count = sent_count + 1 - mine[b]

    def take_swapped(h):
        for t in range(2):
            swap_kv(h, t).wait_recv()
        forward(h, 0, 1 - parity)

    def keys_of(h, t, back, low, high):
        found = []
        for side in range(2):
            begin, end = max(low - side * per, 0), min(high - side * per, per)
            if begin < end:
                at = pl.ds(begin * BLOCK, (end - begin) * BLOCK)
                found.append(kv[h, t, back, side, at])
        return jnp.concatenate(found, axis=0)

    def stages(h, j, own):
        found = [[], [], [], []]
        for back, low, high in spans(j, depth, blocks, reach):
            if back < depth or depth == 0:
                found[0].append((back, low, high))
                continue
            for stage, side in ((1, own), (2, 1 - own)):
                begin, end = max(low, side * per), min(high, (side + 1) * per)
                if begin < end and begin == 0 and is_split(h, back - 1, 0):
                    found[3].append((back, 0, 1))
                    begin = 1
                if begin < end:
                    found[stage].append((back, begin, end))
        return found

    def scored(h, first, j, runs):
        side, inner = j // per, j % per
        at = pl.ds(inner * BLOCK, BLOCK)
        block = jnp.concatenate([q[h, first + g, side, at] for g in range(chunk)], axis=0)
        extra = jnp.concatenate([qext[pl.ds(j * BLOCK, BLOCK)]] * chunk, axis=0)
        grouped = jnp.concatenate([block, extra], axis=1)
        seen = jnp.concatenate(
            [
                jnp.concatenate(
                    [keys_of(h, 0, back, low, high), kext[back, low * BLOCK : high * BLOCK]],
                    axis=1,
                )
                for back, low, high in runs
            ],
            axis=0,
        )
        raw = lax.dot_general(
            grouped, seen, (((1,), (1,)), ((), ())), preferred_element_type=jnp.float32
        )
        parts = []
        begin = 0
        for back, low, high in runs:
            for kb in range(low, high):
                part = raw[:, begin : begin + BLOCK]
                begin += BLOCK
                gap = (back * blocks + j - kb) * BLOCK
                row = lax.broadcasted_iota(jnp.int32, (BLOCK, BLOCK), 0)
                column = lax.broadcasted_iota(jnp.int32, (BLOCK, BLOCK), 1)
                allowed = None
                if gap < BLOCK:
                    allowed = gap + row >= column
                if windowed and gap + BLOCK > WINDOW:
                    allowed = gap + row - column < WINDOW
                if allowed is not None:
                    shaped = part.reshape(chunk, BLOCK, BLOCK)
                    part = jnp.where(allowed[None], shaped, -FAR).reshape(part.shape)
                parts.append(part)
        peak = parts[0]
        for part in parts[1:]:
            peak = jnp.maximum(peak, part)
        return parts, jnp.max(peak, axis=1, keepdims=True)

    def folded(h, parts, peak, runs):
        weights = jnp.concatenate(
            [jnp.exp2((part - peak) * scale).astype(jnp.bfloat16) for part in parts], axis=1
        )
        joined = jnp.concatenate(
            [keys_of(h, 1, back, low, high) for back, low, high in runs], axis=0
        )
        joined = jnp.concatenate([joined, jnp.ones_like(joined)], axis=1)
        return jnp.dot(weights, joined, preferred_element_type=jnp.float32)

    def finish(h, first, j, both):
        result = (both[:, :HD] / both[:, HD:]).astype(mixed.dtype)
        for g in range(chunk):
            mixed[h, first + g, j] = result[g * BLOCK : (g + 1) * BLOCK]

    def attend(h, step, own, begin, end):
        for j in range(blocks):
            found = stages(h, j, own)
            runs = sum(found[begin:end], [])
            if not runs:
                continue
            parts, peak = scored(h, step * chunk, j, runs)
            if begin > 0:
                before = top[step, j]
                peak = jnp.maximum(before, peak)
                rescale = jnp.exp2((before - peak) * scale)
            both = folded(h, parts, peak, runs)
            if begin > 0:
                both = both + part_sum[step, j] * jnp.concatenate([rescale, rescale], axis=1)
            if any(found[end:]):
                top[step, j] = jnp.broadcast_to(peak, top.shape[2:])
                part_sum[step, j] = both
            else:
                finish(h, step * chunk, j, both)

    def by_parity(h, step, begin, end):
        for side in range(2):

            @pl.when(parity == side)
            def _():
                attend(h, step, side, begin, end)

    def deliver(h, first, slots):
        for g in range(chunk):
            for s in slots:
                at = pl.ds(s * BLOCK, BLOCK)
                give[h, first + g, at] = mixed[h, first + g, sent_at[s]]
                keep[h, first + g, at] = mixed[h, first + g, kept_at[s]]
            send_out(h, first + g, slots).start()
            keep_out(h, first + g, slots).start()

    def settle(h, step):
        for g in range(chunk):
            load_q(h, step * chunk + g).wait()
            swap_q(h, step * chunk + g).wait_recv()

    def arrive(h, backs, sides):
        for back in backs:
            for side in sides:
                forward(h, back, side)

    sides = (parity, 1 - parity)
    steps = group // chunk
    soon = range(1, 2 if depth > 1 else 1)
    take_swapped(0)
    arrive(0, soon, sides)
    for h in range(1, halves):
        take_swapped(h)
        arrive(h, soon, sides[:1])
    later = range(soon.stop, depth + 1)
    for h in range(halves):
        if h > 0:
            arrive(h, soon, sides[1:])
        arrive(h, later[:-1], sides)
        if split and h == halves - 1:

            @pl.when((pair >= depth - 1) & (pair < last))
            def _():
                last_hop().start()

        joined = 2 if h == 0 else 1
        if joined == 2:
            arrive(h, later[-1:], sides[:1])

        @pl.loop(0, steps)
        def _(step):
            settle(h, step)
            if joined == 2:
                by_parity(h, step, 0, 2)
            else:
                attend(h, step, 0, 0, 1)

        if joined == 1:
            arrive(h, later[-1:], sides[:1])
        arrive(h, later[-1:], sides[1:])

        @pl.loop(0, steps)
        def _(step):
            if joined == 1:
                attend(h, step, 0, 1, 3)
            else:
                by_parity(h, step, 2, 3)
            deliver(h, step * chunk, batches(h)[0])

        if len(batches(h)) > 1:

            @pl.when(pair >= depth)
            def _():
                last_hop().wait_recv()

            @pl.loop(0, steps)
            def _(step):
                attend(h, step, 0, 3, 4)
                deliver(h, step * chunk, batches(h)[1])

    for h in range(halves):
        for t in range(2):
            swap_kv(h, t).wait_send()
        for back in range(depth):
            for side in range(2):

                @pl.when((pair >= back) & (pair < last))
                def _():
                    each_hop(h, back, side, lambda copy: copy.wait_send())

        for g in range(group):
            swap_q(h, g).wait_send()
            for slots in batches(h):
                keep_out(h, g, slots).wait()
                send_out(h, g, slots).wait()

    if split:

        @pl.when((pair >= depth - 1) & (pair < last))
        def _():
            last_hop().wait_send()


def local(queries, keys, values, lengths, home):
    rows, query_cols = queries.shape
    kv_heads = keys.shape[1] // HD
    group = query_cols // HD // kv_heads
    halves = kv_heads // 2
    blocks = 2 * rows // BLOCK
    seq = lax.axis_size("seq")
    tokens = seq * rows
    most_len = min(tokens // 2, 4096)
    reach = min(WINDOW, most_len)
    depth = min(-(-(reach - 1) // (2 * rows)), seq // 2 - 1)
    plan = (group, halves, depth, reach, most_len > WINDOW, 2)
    bf16 = jnp.bfloat16
    dma = pltpu.SemaphoreType.DMA
    anywhere = pl.BlockSpec(memory_space=pl.ANY)
    hbm = pl.BlockSpec(memory_space=pltpu.HBM)
    return pl.pallas_call(
        functools.partial(fused, plan),
        out_shape=pltpu.VMEM(queries.shape, bf16),
        in_specs=[hbm] * 5,
        out_specs=pl.BlockSpec(memory_space=pltpu.VMEM),
        scratch_shapes=[
            pltpu.SMEM(lengths.shape, jnp.int32),
            pltpu.SMEM(home.shape, jnp.int32),
            pltpu.VMEM((halves, group, 2, rows, HD), bf16),
            pltpu.VMEM((halves, 2, depth + 1, 2, rows, HD), bf16),
            pltpu.VMEM((2 * rows, HD), bf16),
            pltpu.VMEM((depth + 1, 2 * rows, HD), bf16),
            pltpu.VMEM((halves, group, blocks, BLOCK, HD), bf16),
            pltpu.VMEM((halves, group, rows, HD), bf16),
            pltpu.VMEM((halves, group, rows, HD), bf16),
            pltpu.VMEM((group // plan[-1], blocks, plan[-1] * BLOCK, HD), jnp.float32),
            pltpu.VMEM((group // plan[-1], blocks, plan[-1] * BLOCK, 2 * HD), jnp.float32),
            pltpu.SemaphoreType.REGULAR,
            dma((2,)),
            dma((halves, 2)),
            dma((halves, group)),
            dma((halves, group)),
            dma((halves, group)),
            dma((halves, 2)),
            dma((halves, 2)),
            dma((halves, depth, 2, 2)),
            dma((halves, depth, 2, 2)),
            dma((halves, group, rows // BLOCK)),
            dma((halves, group, rows // BLOCK)),
            dma((halves, group, rows // BLOCK)),
        ],
        compiler_params=pltpu.CompilerParams(
            collective_id=0, has_side_effects=True, vmem_limit_bytes=60 * 1024 * 1024
        ),
    )(lengths, home, queries, keys, values)


def solution(mesh):
    placed = (
        P(("pack", "seq"), None),
        P(("pack", "seq"), None),
        P(("pack", "seq"), None),
        P("pack"),
        P("pack"),
    )
    return jax.shard_map(
        local, mesh=mesh, in_specs=placed, out_specs=P(("pack", "seq"), None), check_vma=False
    )
```

```python
import functools

import jax
import jax.numpy as jnp
from jax import lax
from jax.experimental import pallas as pl
from jax.experimental.pallas import tpu as pltpu
from jax.sharding import PartitionSpec as P

HD = 128
BLOCK = 128
WINDOW = 2048
LOG2E = 1.4426950408889634
FAR = float(2**20)
MESH = pl.DeviceIdType.MESH


def spans(row_block, depth, blocks, reach):
    found = []
    for back in range(depth, -1, -1):
        near = [
            kb
            for kb in range(blocks)
            if -BLOCK < (back * blocks + row_block - kb) * BLOCK < reach + BLOCK - 1
        ]
        if near:
            found.append((back, near[0], near[-1] + 1))
    return found


def fused(
    plan, lengths_in, home_in, queries, keys, values, out,
    lengths, home, q, kv, qext, kext, mixed, give, keep, top, part_sum,
    ready, small_sem, load_sem, q_load, q_send, q_recv, kv_send, kv_recv, hop_send, hop_recv, o_send, o_recv, o_keep,
):
    group, halves, depth, reach, windowed, chunk = plan
    rows = queries.shape[0]
    blocks = 2 * rows // BLOCK
    per = blocks // 2
    me = lax.axis_index("seq")
    count = lax.axis_size("seq")
    other = me ^ 1
    parity = me % 2
    pair = me // 2
    last = count // 2 - 1
    scale = HD ** (-0.5) * LOG2E
    far = [j for j in range(blocks) if (depth, 0) in [run[:2] for run in spans(j, depth, blocks, reach)]]
    split = depth > 0 and per > 1 and far == [0]

    def columns(head, wide=1):
        return pl.ds(pl.multiple_of(head * HD, HD), wide * HD)

    def load_kv(h, t):
        source = keys if t == 0 else values
        return pltpu.make_async_copy(
            source.at[:, columns(parity * halves + h)], kv.at[h, t, 0, parity], load_sem.at[h, t]
        )

    def load_q(h, g):
        return pltpu.make_async_copy(
            queries.at[:, columns((parity * halves + h) * group + g)],
            q.at[h, g, parity],
            q_load.at[h, g],
        )

    def swap_kv(h, t):
        source = keys if t == 0 else values
        return pltpu.make_async_remote_copy(
            source.at[:, columns((1 - parity) * halves + h)],
            kv.at[h, t, 0, parity],
            kv_send.at[h, t],
            kv_recv.at[h, t],
            device_id={"seq": other},
            device_id_type=MESH,
        )

    def swap_q(h, g):
        return pltpu.make_async_remote_copy(
            queries.at[:, columns(((1 - parity) * halves + h) * group + g)],
            q.at[h, g, parity],
            q_send.at[h, g],
            q_recv.at[h, g],
            device_id={"seq": other},
            device_id_type=MESH,
        )

    def is_split(h, back, side):
        return split and h == halves - 1 and back == depth - 1 and side == 0

    def hop_rows(h, back, side, begin, end, part):
        return pltpu.make_async_remote_copy(
            kv.at[h, :, back, side, pl.ds(begin, end - begin)],
            kv.at[h, :, back + 1, side, pl.ds(begin, end - begin)],
            hop_send.at[h, back, side, part],
            hop_recv.at[h, back, side, part],
            device_id={"seq": (me + 2) % count},
            device_id_type=MESH,
        )

    def last_hop():
        return hop_rows(halves - 1, depth - 1, 0, 0, BLOCK, 1)

    def each_hop(h, back, side, act):
        if not (split and h == halves - 1 and back == depth - 1):
            act(hop_rows(h, back, side, 0, rows, 0))
            return
        for fixed in range(2):

            @pl.when(side == fixed)
            def _():
                act(hop_rows(h, back, fixed, BLOCK if is_split(h, back, fixed) else 0, rows, 0))

    def out_part(h, g, slots):
        at = pl.ds(slots[0] * BLOCK, len(slots) * BLOCK)
        return at, out.at[at, columns((parity * halves + h) * group + g)]

    def send_out(h, g, slots):
        at, place = out_part(h, g, slots)
        return pltpu.make_async_remote_copy(
            give.at[h, g, at],
            place,
            o_send.at[h, g, slots[0]],
            o_recv.at[h, g, slots[0]],
            device_id={"seq": other},
            device_id_type=MESH,
        )

    def keep_out(h, g, slots):
        at, place = out_part(h, g, slots)
        return pltpu.make_async_copy(keep.at[h, g, at], place, o_keep.at[h, g, slots[0]])

    def batches(h):
        if split and h == halves - 1:
            return [list(range(1, per)), [0]]
        return [list(range(per))]

    def forward(h, back, side):
        if back > 0:

            @pl.when(pair >= back)
            def _():
                each_hop(h, back - 1, side, lambda copy: copy.wait_recv())

        if back < depth:

            @pl.when((pair >= back) & (pair < last))
            def _():
                each_hop(h, back, side, lambda copy: copy.start())

    small = [
        pltpu.make_async_copy(lengths_in, lengths, small_sem.at[0]),
        pltpu.make_async_copy(home_in, home, small_sem.at[1]),
    ]
    for h in range(halves):
        for t in range(2):
            load_kv(h, t).start()
    for copy in small:
        copy.start()
    for h in range(halves):
        for g in range(group):
            load_q(h, g).start()

    barrier = pltpu.get_barrier_semaphore()
    pl.semaphore_signal(barrier, inc=1, device_id={"seq": other}, device_id_type=MESH)

    @pl.when((parity == 0) & (pair > 0))
    def _():
        pl.semaphore_signal(barrier, inc=1, device_id={"seq": me - 2}, device_id_type=MESH)

    @pl.when((parity == 1) & (pair < last))
    def _():
        pl.semaphore_signal(barrier, inc=1, device_id={"seq": me + 2}, device_id_type=MESH)

    greeted = jnp.where(parity == 0, pair < last, pair > 0)
    pl.semaphore_wait(barrier, 1 + greeted.astype(jnp.int32))

    @pl.when((parity == 1) & (pair > 0))
    def _():
        pl.semaphore_signal(ready, inc=1, device_id={"seq": me - 2}, device_id_type=MESH)

    for h in range(halves):
        for t in range(2):
            swap_kv(h, t).start()

    @pl.when((parity == 1) & (pair < last))
    def _():
        pl.semaphore_wait(ready, 1)

    for h in range(halves):
        for t in range(2):
            load_kv(h, t).wait()
        forward(h, 0, parity)
    for h in range(halves):
        for g in range(group):
            swap_q(h, g).start()

    for copy in small:
        copy.wait()

    docs = lengths.shape[0]
    lane = lax.broadcasted_iota(jnp.int32, (8, HD), 1)

    def add_doc(doc, state):
        begin, starts, ends = state
        end = begin + lengths[doc]
        here = lane == doc
        return end, jnp.where(here, begin, starts), jnp.where(here, end, ends)

    nothing = jnp.zeros((8, HD), jnp.int32)
    _, starts, ends = lax.fori_loop(
        0, docs, add_doc, (jnp.int32(0), nothing, nothing), unroll=docs <= 16
    )
    starts, ends = starts[:1], ends[:1]
    offset = lax.broadcasted_iota(jnp.int32, (2 * rows, HD), 0)
    for back in range(depth + 1):
        position = (pair - back) * 2 * rows + offset
        inside = ((position >= starts) & (position < ends)) | (position < 0)
        kext[back] = jnp.where(inside, 1.0, 0.0).astype(kext.dtype)
        if back == 0:
            qext[...] = jnp.where(inside, 0.0, -FAR).astype(qext.dtype)
        else:

            @pl.when(pair < back)
            def _():
                for h in range(halves):
                    kv[h, :, back] = jnp.zeros(kv.shape[1:2] + kv.shape[3:], kv.dtype)

    mine = [(home[pair * blocks + b] == me).astype(jnp.int32) for b in range(blocks)]
    kept_at = [jnp.int32(0)] * per
    sent_at = [jnp.int32(0)] * per
    kept_count, sent_count = jnp.int32(0), jnp.int32(0)
    for b in range(blocks):
        for s in range(per):
            kept_at[s] = jnp.where((mine[b] == 1) & (kept_count == s), b, kept_at[s])
            sent_at[s] = jnp.where((mine[b] == 0) & (sent_count == s), b, sent_at[s])
        kept_count = kept_count + mine[b]
        sent_count = sent_count + 1 - mine[b]

    def take_swapped(h):
        for t in range(2):
            swap_kv(h, t).wait_recv()
        forward(h, 0, 1 - parity)

    def keys_of(h, t, back, low, high):
        found = []
        for side in range(2):
            begin, end = max(low - side * per, 0), min(high - side * per, per)
            if begin < end:
                at = pl.ds(begin * BLOCK, (end - begin) * BLOCK)
                found.append(kv[h, t, back, side, at])
        return jnp.concatenate(found, axis=0)

    def stages(h, j, own):
        found = [[], [], [], []]
        for back, low, high in spans(j, depth, blocks, reach):
            if back < depth or depth == 0:
                found[0].append((back, low, high))
                continue
            for stage, side in ((1, own), (2, 1 - own)):
                begin, end = max(low, side * per), min(high, (side + 1) * per)
                if begin < end and begin == 0 and is_split(h, back - 1, 0):
                    found[3].append((back, 0, 1))
                    begin = 1
                if begin < end:
                    found[stage].append((back, begin, end))
        return found

    def scored(h, first, j, runs):
        side, inner = j // per, j % per
        at = pl.ds(inner * BLOCK, BLOCK)
        block = jnp.concatenate([q[h, first + g, side, at] for g in range(chunk)], axis=0)
        extra = jnp.concatenate([qext[pl.ds(j * BLOCK, BLOCK)]] * chunk, axis=0)
        grouped = jnp.concatenate([block, extra], axis=1)
        seen = jnp.concatenate(
            [
                jnp.concatenate(
                    [keys_of(h, 0, back, low, high), kext[back, low * BLOCK : high * BLOCK]],
                    axis=1,
                )
                for back, low, high in runs
            ],
            axis=0,
        )
        raw = lax.dot_general(
            grouped, seen, (((1,), (1,)), ((), ())), preferred_element_type=jnp.float32
        )
        parts = []
        begin = 0
        for back, low, high in runs:
            for kb in range(low, high):
                part = raw[:, begin : begin + BLOCK]
                begin += BLOCK
                gap = (back * blocks + j - kb) * BLOCK
                row = lax.broadcasted_iota(jnp.int32, (BLOCK, BLOCK), 0)
                column = lax.broadcasted_iota(jnp.int32, (BLOCK, BLOCK), 1)
                allowed = None
                if gap < BLOCK:
                    allowed = gap + row >= column
                if windowed and gap + BLOCK > WINDOW:
                    allowed = gap + row - column < WINDOW
                if allowed is not None:
                    shaped = part.reshape(chunk, BLOCK, BLOCK)
                    part = jnp.where(allowed[None], shaped, -FAR).reshape(part.shape)
                parts.append(part)
        peak = parts[0]
        for part in parts[1:]:
            peak = jnp.maximum(peak, part)
        return parts, jnp.max(peak, axis=1, keepdims=True)

    def folded(h, parts, peak, runs):
        weights = jnp.concatenate(
            [jnp.exp2((part - peak) * scale).astype(jnp.bfloat16) for part in parts], axis=1
        )
        joined = jnp.concatenate(
            [keys_of(h, 1, back, low, high) for back, low, high in runs], axis=0
        )
        joined = jnp.concatenate([joined, jnp.ones_like(joined)], axis=1)
        return jnp.dot(weights, joined, preferred_element_type=jnp.float32)

    def finish(h, first, j, both):
        result = (both[:, :HD] / both[:, HD:]).astype(mixed.dtype)
        for g in range(chunk):
            mixed[h, first + g, j] = result[g * BLOCK : (g + 1) * BLOCK]

    def attend(h, step, own, begin, end):
        for j in range(blocks):
            found = stages(h, j, own)
            runs = sum(found[begin:end], [])
            if not runs:
                continue
            parts, peak = scored(h, step * chunk, j, runs)
            if begin > 0:
                before = top[step, j]
                peak = jnp.maximum(before, peak)
                rescale = jnp.exp2((before - peak) * scale)
            both = folded(h, parts, peak, runs)
            if begin > 0:
                both = both + part_sum[step, j] * jnp.concatenate([rescale, rescale], axis=1)
            if any(found[end:]):
                top[step, j] = jnp.broadcast_to(peak, top.shape[2:])
                part_sum[step, j] = both
            else:
                finish(h, step * chunk, j, both)

    def by_parity(h, step, begin, end):
        for side in range(2):

            @pl.when(parity == side)
            def _():
                attend(h, step, side, begin, end)

    def deliver(h, first, slots):
        for g in range(chunk):
            for s in slots:
                at = pl.ds(s * BLOCK, BLOCK)
                give[h, first + g, at] = mixed[h, first + g, sent_at[s]]
                keep[h, first + g, at] = mixed[h, first + g, kept_at[s]]
            send_out(h, first + g, slots).start()
            keep_out(h, first + g, slots).start()

    def settle(h, step):
        for g in range(chunk):
            load_q(h, step * chunk + g).wait()
            swap_q(h, step * chunk + g).wait_recv()

    def arrive(h, backs, sides):
        for back in backs:
            for side in sides:
                forward(h, back, side)

    sides = (parity, 1 - parity)
    steps = group // chunk
    soon = range(1, 2 if depth > 1 else 1)
    take_swapped(0)
    arrive(0, soon, sides)
    for h in range(1, halves):
        take_swapped(h)
        arrive(h, soon, sides[:1])
    later = range(soon.stop, depth + 1)
    for h in range(halves):
        if h > 0:
            arrive(h, soon, sides[1:])
        arrive(h, later[:-1], sides)
        if split and h == halves - 1:

            @pl.when((pair >= depth - 1) & (pair < last))
            def _():
                last_hop().start()

        joined = 2 if h == 0 else 1
        if joined == 2:
            arrive(h, later[-1:], sides[:1])

        @pl.loop(0, steps)
        def _(step):
            settle(h, step)
            if joined == 2:
                by_parity(h, step, 0, 2)
            else:
                attend(h, step, 0, 0, 1)

        if joined == 1:
            arrive(h, later[-1:], sides[:1])
        arrive(h, later[-1:], sides[1:])

        @pl.loop(0, steps)
        def _(step):
            if joined == 1:
                attend(h, step, 0, 1, 3)
            else:
                by_parity(h, step, 2, 3)
            deliver(h, step * chunk, batches(h)[0])

        if len(batches(h)) > 1:

            @pl.when(pair >= depth)
            def _():
                last_hop().wait_recv()

            @pl.loop(0, steps)
            def _(step):
                attend(h, step, 0, 3, 4)
                deliver(h, step * chunk, batches(h)[1])

    for h in range(halves):
        for t in range(2):
            swap_kv(h, t).wait_send()
        for back in range(depth):
            for side in range(2):

                @pl.when((pair >= back) & (pair < last))
                def _():
                    each_hop(h, back, side, lambda copy: copy.wait_send())

        for g in range(group):
            swap_q(h, g).wait_send()
            for slots in batches(h):
                keep_out(h, g, slots).wait()
                send_out(h, g, slots).wait()

    if split:

        @pl.when((pair >= depth - 1) & (pair < last))
        def _():
            last_hop().wait_send()


def local(queries, keys, values, lengths, home):
    rows, query_cols = queries.shape
    kv_heads = keys.shape[1] // HD
    group = query_cols // HD // kv_heads
    halves = kv_heads // 2
    blocks = 2 * rows // BLOCK
    seq = lax.axis_size("seq")
    tokens = seq * rows
    most_len = min(tokens // 2, 4096)
    reach = min(WINDOW, most_len)
    depth = min(-(-(reach - 1) // (2 * rows)), seq // 2 - 1)
    plan = (group, halves, depth, reach, most_len > WINDOW, 2)
    bf16 = jnp.bfloat16
    dma = pltpu.SemaphoreType.DMA
    anywhere = pl.BlockSpec(memory_space=pl.ANY)
    hbm = pl.BlockSpec(memory_space=pltpu.HBM)
    return pl.pallas_call(
        functools.partial(fused, plan),
        out_shape=pltpu.VMEM(queries.shape, bf16),
        in_specs=[hbm] * 5,
        out_specs=pl.BlockSpec(memory_space=pltpu.VMEM),
        scratch_shapes=[
            pltpu.SMEM(lengths.shape, jnp.int32),
            pltpu.SMEM(home.shape, jnp.int32),
            pltpu.VMEM((halves, group, 2, rows, HD), bf16),
            pltpu.VMEM((halves, 2, depth + 1, 2, rows, HD), bf16),
            pltpu.VMEM((2 * rows, HD), bf16),
            pltpu.VMEM((depth + 1, 2 * rows, HD), bf16),
            pltpu.VMEM((halves, group, blocks, BLOCK, HD), bf16),
            pltpu.VMEM((halves, group, rows, HD), bf16),
            pltpu.VMEM((halves, group, rows, HD), bf16),
            pltpu.VMEM((group // plan[-1], blocks, plan[-1] * BLOCK, HD), jnp.float32),
            pltpu.VMEM((group // plan[-1], blocks, plan[-1] * BLOCK, 2 * HD), jnp.float32),
            pltpu.SemaphoreType.REGULAR,
            dma((2,)),
            dma((halves, 2)),
            dma((halves, group)),
            dma((halves, group)),
            dma((halves, group)),
            dma((halves, 2)),
            dma((halves, 2)),
            dma((halves, depth, 2, 2)),
            dma((halves, depth, 2, 2)),
            dma((halves, group, rows // BLOCK)),
            dma((halves, group, rows // BLOCK)),
            dma((halves, group, rows // BLOCK)),
        ],
        compiler_params=pltpu.CompilerParams(
            collective_id=0, has_side_effects=True, vmem_limit_bytes=60 * 1024 * 1024
        ),
    )(lengths, home, queries, keys, values)


def solution(mesh):
    placed = (
        P(("pack", "seq"), None),
        P(("pack", "seq"), None),
        P(("pack", "seq"), None),
        P("pack"),
        P("pack"),
    )
    return jax.shard_map(
        local, mesh=mesh, in_specs=placed, out_specs=P(("pack", "seq"), None), check_vma=False
    )
```
